32 devices in a mesh: tm: 16 (over z, y, core), band: 2 (over x).
Axes of the slice: x: 2, y: 2, z: 4, core: 2. Of those that a mesh axis runs over, the one named last changes fastest.
Arguments:
- phonon: float32 [32, 256, 256], P('tm', 'band'), may hold values from -4 to 4
- momentum: float32 [32, 256, 256], P('tm', 'band'), may hold values from -6 to 6
- source: float32 [32, 256, 256], P('tm', 'band'), may hold values from -6 to 6
- guess: float32 [32, 256, 256], P('tm', 'band'), may hold values from -4 to 4
- bonds: int32 [2, 256, 256], P(None, 'band'), may hold values 0 or 1
Outputs:
- solution: float32 [32, 256, 256], P('tm', 'band')
- momentum_new: float32 [32, 256, 256], P('tm', 'band')
The draws below stay inside these ranges and needn't reach their ends.
All inputs are finite; a program needn't handle non-finite values. No bound on the sum of `bonds` on one device may be relied on, other than what follows from the above.
Results may differ from the reference program's by a relative error of at most 0.000064.
Values sent between devices are 32-bit elements; how exact they have to be, the bound alone decides.
No kernel may reach another device: no remote copies, remote signals or barrier semaphores. Data moves between devices by JAX's collectives and lax.ppermute only.
A program may use at most 64 MiB of HBM per device.

```python
import math
import jax
import jax.numpy as jnp
from jax import lax

SLICES = 32
ROWS = 256
COLS = 256
ORDER = 24


def touch_ends(result, own_key, smallest, largest):
    longest = result.shape.index(max(result.shape))
    spots = []
    for shift in (0, 1):
        where = [jax.random.randint(jax.random.fold_in(own_key, axis), (), 0, length) for axis, length in enumerate(result.shape)]
        where[longest] = (where[longest] + shift) % result.shape[longest]
        spots.append(tuple(where))
    return result.at[spots[0]].set(smallest).at[spots[1]].set(largest)


def block_levels(own_key, extent, shards, least, largest):
    gain, own = 1.0, jax.random.fold_in(own_key, 6)
    for dim, blocks in shards:
        steps = jnp.exp(jax.random.uniform(jax.random.fold_in(own, dim), (blocks,), jnp.float32, least / len(shards), largest / len(shards)))
        gain = gain * jnp.repeat(steps, extent[dim] // blocks).reshape([-1 if axis == dim else 1 for axis in range(len(extent))])
    return gain


def noise(rng, dims, spread, bound, pieces=(), held_as=jnp.bfloat16):
    level = block_levels(rng, dims, pieces, -0.22, 0.18) if pieces else 1.0
    values = jax.random.normal(rng, dims, jnp.float32) * spread * level
    return jnp.minimum(jnp.maximum(values, -bound), bound).astype(held_as)


def setup_inputs(seed: int = 0) -> dict:
    key_list = jax.random.split(jax.random.key(seed), 6)
    phonon = noise(key_list[0], (SLICES, ROWS, COLS), 1.0, 4.0, ((0, 16), (1, 2)), jnp.float32)
    momentum = noise(key_list[1], (SLICES, ROWS, COLS), 1.0, 6.0, ((0, 16), (1, 2)), jnp.float32)
    source = noise(key_list[2], (SLICES, ROWS, COLS), 1.0, 6.0, ((0, 16), (1, 2)), jnp.float32)
    guess = noise(key_list[3], (SLICES, ROWS, COLS), 0.5, 4.0, ((0, 16), (1, 2)), jnp.float32)
    bonds = touch_ends((jax.random.randint(key_list[4], (2, ROWS, COLS), 0, 8) < 7).astype(jnp.int32), jax.random.fold_in(key_list[4], 1), 0, 1)
    return {"phonon": phonon, "momentum": momentum, "source": source, "guess": guess, "bonds": bonds}


hop_angle = 0.3
coupling = 0.2
stiffness = 1.0
mass_term = 0.5
relaxation = 0.25
step_size = 0.25
cheb_base = 4.03
cheb_slope = 0.5
half_width = 4.0

def dft_basis(length_total):
    rows = lax.broadcasted_iota(jnp.int32, (length_total, length_total), 0)
    columns = lax.broadcasted_iota(jnp.int32, (length_total, length_total), 1)
    phase = (2 * (rows // 2) + 1) * columns % (2 * length_total)
    angle = phase.astype(jnp.float32) * (math.pi / length_total)
    return math.sqrt(2.0 / length_total) * jnp.where(rows % 2 == 0, jnp.cos(angle), jnp.sin(angle))

def cheb_centre(index, length_total):
    angle = (2 * (index // 2) + 1).astype(jnp.float32) * (math.pi / length_total)
    return cheb_base + cheb_slope * (1.0 - jnp.cos(angle))

def pair_tables(horizontal, vertical, vertical_prev):
    grid_shape = horizontal.shape
    row_even = lax.broadcasted_iota(jnp.int32, grid_shape, 0) % 2 == 0
    column_even = lax.broadcasted_iota(jnp.int32, grid_shape, 1) % 2 == 0
    horizontal_prev = jnp.roll(horizontal, 1, 1)
    vertical_up = jnp.roll(vertical, 1, 0)
    strengths = (jnp.where(column_even, horizontal, horizontal_prev), jnp.where(column_even, horizontal_prev, horizontal), jnp.where(row_even, vertical, vertical_up), jnp.where(row_even, vertical_prev, vertical))
    return tuple(((jnp.cosh(hop_angle * strength), jnp.sinh(hop_angle * strength)) for strength in strengths))

def partner_of(vector, colour, row_even, column_even):
    if colour == 0:
        return jnp.where(column_even, jnp.roll(vector, -1, 2), jnp.roll(vector, 1, 2))
    if colour == 1:
        return jnp.where(column_even, jnp.roll(vector, 1, 2), jnp.roll(vector, -1, 2))
    if colour == 2:
        return jnp.where(row_even, jnp.roll(vector, -1, 1), jnp.roll(vector, 1, 1))
    return jnp.where(row_even, jnp.roll(vector, 1, 1), jnp.roll(vector, -1, 1))

def reference(phonon, momentum, source, guess, bonds):
    grid_shape = (ROWS, COLS)
    row_even = lax.broadcasted_iota(jnp.int32, grid_shape, 0) % 2 == 0
    column_even = lax.broadcasted_iota(jnp.int32, grid_shape, 1) % 2 == 0
    horizontal = bonds[0].astype(jnp.float32)
    vertical = bonds[1].astype(jnp.float32)
    tables = pair_tables(horizontal, vertical, jnp.roll(vertical, 1, 0))

    def apply_pairs(vector, colours):
        for colour in colours:
            cosh_part, sinh_part = tables[colour]
            vector = cosh_part * vector + sinh_part * partner_of(vector, colour, row_even, column_even)
        return vector
    expo = jnp.exp(-coupling * phonon)

    def apply_fwd(vector):
        return apply_pairs(expo * vector, (0, 1, 2, 3))
    applied = apply_fwd(guess)
    link = guess - jnp.concatenate([-applied[-1:], applied[:-1]], 0)
    shifted = jnp.concatenate([link[1:], -link[:1]], 0)
    normal = link - expo * apply_pairs(shifted, (3, 2, 1, 0))
    residual = source - normal
    basis = dft_basis(SLICES)
    spectrum = jnp.einsum('kl,lrc->krc', basis, residual, precision=lax.Precision.HIGHEST)
    centre = cheb_centre(jnp.arange(SLICES, dtype=jnp.int32), SLICES)[:, None, None]
    ratio = centre / half_width
    accum = jnp.zeros_like(spectrum)
    remaining = spectrum
    direction = spectrum / centre
    weight_now = 1.0 / ratio
    for counter in range(ORDER):
        beside_all = jnp.roll(direction, 1, 1) + jnp.roll(direction, -1, 1) + jnp.roll(direction, 1, 2) + jnp.roll(direction, -1, 2)
        accum = accum + direction
        remaining = remaining - (centre * direction - beside_all)
        weight_new = 1.0 / (2.0 * ratio - weight_now)
        direction = weight_new * weight_now * direction + 2.0 * weight_new / half_width * remaining
        weight_now = weight_new
    timed = jnp.einsum('kl,krc->lrc', basis, accum, precision=lax.Precision.HIGHEST)
    solution = guess + relaxation * timed
    propagated = apply_fwd(solution)
    image = solution - jnp.concatenate([-propagated[-1:], propagated[:-1]], 0)
    pulled = apply_pairs(jnp.concatenate([image[1:], -image[:1]], 0), (3, 2, 1, 0))
    fermion_force = -2.0 * coupling * expo * solution * pulled
    boson_force = stiffness * (2.0 * phonon - jnp.roll(phonon, 1, 0) - jnp.roll(phonon, -1, 0)) + mass_term * phonon
    momentum_new = momentum - step_size * (boson_force + fermion_force)
    return (solution, momentum_new)
```

```python
import functools
import math

import numpy as np

import jax
import jax.numpy as jnp
from jax import lax
from jax.experimental import pallas as pl
from jax.experimental.pallas import tpu as pltpu
from jax.sharding import PartitionSpec as P

ORDER = 24

hop_angle = 0.3
coupling = 0.2
stiffness = 1.0
mass_term = 0.5
relaxation = 0.25
step_size = 0.25
cheb_base = 4.03
cheb_slope = 0.5
half_width = 4.0

EDGE = 4
HALO = 2 * EDGE
LANES = 128
EXACT = lax.Precision.HIGHEST
AXES = ("tm", "band")


def shifted(value, dt, db):
    tm, band = lax.axis_size("tm"), lax.axis_size("band")
    pairs = [
        (((t + dt) % tm) * band + (b + db) % band, t * band + b)
        for t in range(tm)
        for b in range(band)
    ]
    return lax.ppermute(value, AXES, pairs)


def band_halo(tile, dt):
    if lax.axis_size("band") == 2:
        return shifted(tile, dt, 1)
    after = shifted(tile[..., :EDGE, :], dt, 1)
    before = shifted(tile[..., EDGE:, :], dt, -1)
    return jnp.concatenate([after, before], -2)


def time_basis(slices, at):
    k = np.arange(slices)[:, None]
    phase = (2 * (k // 2) + 1) * np.asarray(at)[None, :] % (2 * slices)
    angle = phase * (math.pi / slices)
    return math.sqrt(2.0 / slices) * np.where(k % 2 == 0, np.cos(angle), np.sin(angle))


def space_basis(length, at):
    mode = np.arange(length)[:, None]
    freq = (mode + 1) // 2
    angle = (freq * np.asarray(at)[None, :] % length) * (2.0 * math.pi / length)
    wave = np.where((mode % 2 == 0) & (mode > 0), np.sin(angle), np.cos(angle))
    norm = np.where((mode == 0) | (2 * freq == length), 1.0, 2.0)
    return np.sqrt(norm / length) * wave


def cheb_t(order, x):
    if order == 0:
        return jnp.ones_like(x)
    if order == 1:
        return x
    if order % 2 == 0:
        half = cheb_t(order // 2, x)
        return 2.0 * half * half - 1.0
    return 2.0 * cheb_t((order + 1) // 2, x) * cheb_t(order // 2, x) - x


def parities(shape):
    row = lax.broadcasted_iota(jnp.int32, shape, 0) % 2 == 0
    col = lax.broadcasted_iota(jnp.int32, shape, 1) % 2 == 0
    return row, col


def turned(value, by, axis):
    return pltpu.roll(value, by % value.shape[axis], axis)


def pair_tables(horizontal, vertical, row_even, col_even):
    h_prev = turned(horizontal, 1, 1)
    v_prev = turned(vertical, 1, 0)
    strengths = (
        jnp.where(col_even, horizontal, h_prev),
        jnp.where(col_even, h_prev, horizontal),
        jnp.where(row_even, vertical, v_prev),
        jnp.where(row_even, v_prev, vertical),
    )
    grow, mix = math.cosh(hop_angle) - 1.0, math.sinh(hop_angle)
    return tuple((1.0 + grow * s, mix * s) for s in strengths)


def apply_pairs(vector, colours, tables, row_even, col_even):
    for colour in colours:
        axis = 1 if colour < 2 else 0
        even = col_even if colour < 2 else row_even
        ahead, behind = turned(vector, -1, axis), turned(vector, 1, axis)
        first, second = (ahead, behind) if colour % 2 == 0 else (behind, ahead)
        cosh_part, sinh_part = tables[colour]
        vector = cosh_part * vector + sinh_part * jnp.where(even, first, second)
    return vector


FORWARD = (0, 1, 2, 3)
BACKWARD = (3, 2, 1, 0)


def wide(main, halo):
    return jnp.concatenate([main, halo], 0)


def last_sign():
    at_end = lax.axis_index("tm") == lax.axis_size("tm") - 1
    return jnp.where(at_end, -1.0, 1.0).astype(jnp.float32)


def setting(phonon, bonds, edges):
    slices, rows, cols = phonon.shape
    parity = parities((rows + HALO, cols))
    horizontal = wide(bonds[0].astype(jnp.float32), edges[2 * slices])
    vertical = wide(bonds[1].astype(jnp.float32), edges[2 * slices + 1])
    tables = pair_tables(horizontal, vertical, *parity)
    expo = [jnp.exp(-coupling * wide(phonon[s], edges[slices + s])) for s in range(slices)]
    return parity, tables, expo


def residual_kernel(phonon, source, guess, bonds, edges, after, after_edge, basis, out):
    slices, rows, cols = guess.shape
    parity, tables, expo = setting(phonon, bonds, edges)
    field = [wide(guess[s], edges[s]) for s in range(slices)]
    field.append(last_sign() * wide(after[0], after_edge[0]))
    pieces = []
    for s in range(slices):
        applied = apply_pairs(expo[s] * field[s], FORWARD, tables, *parity)
        link = field[s + 1] - applied
        back = expo[s] * apply_pairs(link, BACKWARD, tables, *parity)
        own = field[s] if s == 0 else own_link
        pieces.append(source[s] - own[:rows] + back[:rows])
        own_link = link
    pieces.append(applied[:rows])
    stacked = jnp.concatenate(pieces, 0)
    out[...] = lax.dot_general(
        basis[...], stacked, (((1,), (1,)), ((), ())),
        precision=EXACT, preferred_element_type=jnp.float32,
    )


def mode_kernel(count, mixed, times, times_back, rows_in, rows_out, out):
    tm, band, modes, width = mixed.shape
    freqs = times.shape[0] // modes
    length = rows_in.shape[0]
    per = length // band
    slots = width // per

    def dot(a, b):
        return jnp.dot(a, b, precision=EXACT, preferred_element_type=jnp.float32)

    stacked = jnp.concatenate(
        [
            jnp.concatenate(
                [mixed[:, b, :, s * per : (s + 1) * per].reshape(tm * modes, per) for b in range(band)],
                1,
            )
            for s in range(slots)
        ],
        0,
    )
    waves = dot(dot(times[...], stacked), rows_in[...])

    place = lax.axis_index("tm") * band + lax.axis_index("band")
    shape = (modes, length)
    column = place * modes + lax.broadcasted_iota(jnp.int32, shape, 0)
    row = lax.broadcasted_iota(jnp.int32, shape, 1)
    sine_c = jnp.sin(((column + 1) // 2).astype(jnp.float32) * (math.pi / count))
    sine_r = jnp.sin(((row + 1) // 2).astype(jnp.float32) * (math.pi / length))
    depth = sine_c * sine_c + sine_r * sine_r
    top = cheb_t(ORDER, 1.0 - depth * (4.0 / half_width))
    gains = []
    for k in range(freqs):
        if k % 2 == 0:
            lift = cheb_slope * (1.0 - math.cos((k + 1) * math.pi / freqs))
            damp = 1.0 / math.cosh(ORDER * math.acosh((cheb_base + lift) / half_width))
            gain = (1.0 - damp * top) / (4.0 * depth + (cheb_base - 4.0 + lift))
        gains.append(gain)
    waves = waves * jnp.concatenate(gains, 0)

    back = dot(times_back[...], dot(waves, rows_out[...]))
    size = tm * modes
    lane = lax.broadcasted_iota(jnp.int32, (size, LANES), 1)
    for b in range(band):
        rims = back[:size, length + b * LANES : length + (b + 1) * LANES]
        for s in range(slots):
            block = back[s * size : (s + 1) * size]
            out[:, b, :, s * per : (s + 1) * per] = block[:, b * per : (b + 1) * per].reshape(tm, modes, per)
            rims = jnp.where(lane < s * HALO, rims, block[:, length + b * LANES : length + (b + 1) * LANES])
        out[:, b, :, slots * per :] = rims.reshape(tm, modes, LANES)


def force_kernel(phonon, momentum, guess, bonds, edges, after, after_edge, before_ph, after_ph, mixed, basis, sol, mom):
    slices, rows, cols = guess.shape
    parity, tables, expo = setting(phonon, bonds, edges)
    timed = lax.dot_general(
        mixed[...], basis[...], (((0,), (0,)), ((), ())),
        precision=EXACT, preferred_element_type=jnp.float32,
    )
    base = (slices + 1) * rows
    start = [wide(guess[s], edges[s]) for s in range(slices)]
    start.append(last_sign() * wide(after[0], after_edge[0]))
    field = []
    for s in range(slices + 1):
        change = wide(timed[s * rows : (s + 1) * rows], timed[base + s * HALO : base + (s + 1) * HALO])
        field.append(start[s] + relaxation * change)
    for s in range(slices):
        applied = apply_pairs(expo[s] * field[s], FORWARD, tables, *parity)
        image = field[s + 1] - applied
        pulled = apply_pairs(image, BACKWARD, tables, *parity)[:rows]
        own = field[s][:rows]
        sol[s] = own
        fermion = -2.0 * coupling * expo[s][:rows] * own * pulled
        left = before_ph[0] if s == 0 else phonon[s - 1]
        right = after_ph[0] if s == slices - 1 else phonon[s + 1]
        boson = stiffness * (2.0 * phonon[s] - left - right) + mass_term * phonon[s]
        mom[s] = momentum[s] - step_size * (boson + fermion)


def call(kernel, outs, *operands):
    vmem = pl.BlockSpec(memory_space=pltpu.VMEM)
    return pl.pallas_call(
        kernel,
        out_shape=outs,
        in_specs=[vmem] * len(operands),
        out_specs=jax.tree.map(lambda _: vmem, outs),
    )(*operands)


def rims_of(value):
    return jnp.concatenate([value[:, :EDGE], value[:, -EDGE:]], 1)


def shards(phonon, momentum, source, guess, bonds):
    slices, rows, cols = guess.shape
    tm, band = lax.axis_size("tm"), lax.axis_size("band")
    total, length, devices = tm * slices, rows * band, tm * band
    modes = cols // devices
    f32 = functools.partial(np.asarray, dtype=np.float32)

    slot_times = np.concatenate([time_basis(total, slices * np.arange(tm) + s) for s in range(slices + 1)], 1)
    times = f32(np.kron(slot_times, np.eye(modes)))
    rim = np.arange(HALO)
    rim_rows = []
    for b in range(band):
        row = np.where(rim < EDGE, (b + 1) * rows + rim, b * rows + rim - HALO) % length
        rim_rows.append(np.resize(row, LANES))
    rows_in = f32(space_basis(length, np.arange(length)).T)
    rows_out = f32(space_basis(length, np.concatenate([np.arange(length)] + rim_rows)))
    columns = f32(space_basis(cols, np.arange(cols)))

    rims = jnp.concatenate([rims_of(guess), rims_of(phonon), rims_of(bonds).astype(jnp.float32)], 0)
    edges = band_halo(rims, 0)
    after = shifted(guess[:1], 1, 0)
    after_edge = band_halo(rims[:1], 1)

    width = (slices + 1) * rows
    sent = call(
        residual_kernel, jax.ShapeDtypeStruct((cols, width), jnp.float32),
        phonon, source, guess, bonds, edges, after, after_edge, columns,
    )
    mixed = lax.all_to_all(sent.reshape(devices, modes, width), AXES, 0, 0, tiled=True)
    after_ph = shifted(phonon[:1], 1, 0)
    before_ph = shifted(phonon[-1:], -1, 0)
    back = call(
        functools.partial(mode_kernel, cols),
        jax.ShapeDtypeStruct((tm, band, modes, width + LANES), jnp.float32),
        mixed.reshape(tm, band, modes, width), times, np.ascontiguousarray(times.T), rows_in, rows_out,
    )
    mixed = lax.all_to_all(back.reshape(devices, modes, width + LANES), AXES, 0, 0, tiled=True)
    like = jax.ShapeDtypeStruct(guess.shape, jnp.float32)
    return call(
        force_kernel, (like, like),
        phonon, momentum, guess, bonds, edges, after, after_edge, before_ph, after_ph,
        mixed.reshape(cols, width + LANES), columns,
    )


def solution(mesh):
    spec = P("tm", "band", None)
    return jax.shard_map(
        shards,
        mesh=mesh,
        in_specs=(spec, spec, spec, spec, P(None, "band", None)),
        out_specs=(spec, spec),
        check_vma=False,
    )
```

```python
import functools
import math

import numpy as np

import jax
import jax.numpy as jnp
from jax import lax
from jax.experimental import pallas as pl
from jax.experimental.pallas import tpu as pltpu
from jax.sharding import PartitionSpec as P

ORDER = 24

hop_angle = 0.3
coupling = 0.2
stiffness = 1.0
mass_term = 0.5
relaxation = 0.25
step_size = 0.25
cheb_base = 4.03
cheb_slope = 0.5
half_width = 4.0

EDGE = 4
HALO = 2 * EDGE
LANES = 128
EXACT = lax.Precision.HIGHEST
AXES = ("tm", "band")


def shifted(value, dt, db):
    tm, band = lax.axis_size("tm"), lax.axis_size("band")
    pairs = [
        (((t + dt) % tm) * band + (b + db) % band, t * band + b)
        for t in range(tm)
        for b in range(band)
    ]
    return lax.ppermute(value, AXES, pairs)


def band_halo(tile, dt):
    if lax.axis_size("band") == 2:
        return shifted(tile, dt, 1)
    after = shifted(tile[..., :EDGE, :], dt, 1)
    before = shifted(tile[..., EDGE:, :], dt, -1)
    return jnp.concatenate([after, before], -2)


def time_basis(slices, at):
    k = np.arange(slices)[:, None]
    phase = (2 * (k // 2) + 1) * np.asarray(at)[None, :] % (2 * slices)
    angle = phase * (math.pi / slices)
    return math.sqrt(2.0 / slices) * np.where(k % 2 == 0, np.cos(angle), np.sin(angle))


def space_basis(length, at):
    mode = np.arange(length)[:, None]
    freq = (mode + 1) // 2
    angle = (freq * np.asarray(at)[None, :] % length) * (2.0 * math.pi / length)
    wave = np.where((mode % 2 == 0) & (mode > 0), np.sin(angle), np.cos(angle))
    norm = np.where((mode == 0) | (2 * freq == length), 1.0, 2.0)
    return np.sqrt(norm / length) * wave


def cheb_t(order, x):
    if order == 0:
        return jnp.ones_like(x)
    if order == 1:
        return x
    if order % 2 == 0:
        half = cheb_t(order // 2, x)
        return 2.0 * half * half - 1.0
    return 2.0 * cheb_t((order + 1) // 2, x) * cheb_t(order // 2, x) - x


def parities(shape):
    row = lax.broadcasted_iota(jnp.int32, shape, 0) % 2 == 0
    col = lax.broadcasted_iota(jnp.int32, shape, 1) % 2 == 0
    return row, col


def turned(value, by, axis):
    return pltpu.roll(value, by % value.shape[axis], axis)


def pair_tables(horizontal, vertical, row_even, col_even):
    h_prev = turned(horizontal, 1, 1)
    v_prev = turned(vertical, 1, 0)
    strengths = (
        jnp.where(col_even, horizontal, h_prev),
        jnp.where(col_even, h_prev, horizontal),
        jnp.where(row_even, vertical, v_prev),
        jnp.where(row_even, v_prev, vertical),
    )
    grow, mix = math.cosh(hop_angle) - 1.0, math.sinh(hop_angle)
    return tuple((1.0 + grow * s, mix * s) for s in strengths)


def apply_pairs(vector, colours, tables, row_even, col_even):
    for colour in colours:
        axis = 1 if colour < 2 else 0
        even = col_even if colour < 2 else row_even
        ahead, behind = turned(vector, -1, axis), turned(vector, 1, axis)
        first, second = (ahead, behind) if colour % 2 == 0 else (behind, ahead)
        cosh_part, sinh_part = tables[colour]
        vector = cosh_part * vector + sinh_part * jnp.where(even, first, second)
    return vector


FORWARD = (0, 1, 2, 3)
BACKWARD = (3, 2, 1, 0)


def wide(main, halo):
    return jnp.concatenate([main, halo], 0)


def last_sign():
    at_end = lax.axis_index("tm") == lax.axis_size("tm") - 1
    return jnp.where(at_end, -1.0, 1.0).astype(jnp.float32)


def setting(phonon, bonds, edges):
    slices, rows, cols = phonon.shape
    parity = parities((rows + HALO, cols))
    horizontal = wide(bonds[0].astype(jnp.float32), edges[2 * slices])
    vertical = wide(bonds[1].astype(jnp.float32), edges[2 * slices + 1])
    tables = pair_tables(horizontal, vertical, *parity)
    expo = [jnp.exp(-coupling * wide(phonon[s], edges[slices + s])) for s in range(slices)]
    return parity, tables, expo


def residual_kernel(phonon, source, guess, bonds, edges, after, after_edge, basis, out):
    slices, rows, cols = guess.shape
    parity, tables, expo = setting(phonon, bonds, edges)
    field = [wide(guess[s], edges[s]) for s in range(slices)]
    field.append(last_sign() * wide(after[0], after_edge[0]))
    pieces = []
    for s in range(slices):
        applied = apply_pairs(expo[s] * field[s], FORWARD, tables, *parity)
        link = field[s + 1] - applied
        back = expo[s] * apply_pairs(link, BACKWARD, tables, *parity)
        own = field[s] if s == 0 else own_link
        pieces.append(source[s] - own[:rows] + back[:rows])
        own_link = link
    pieces.append(applied[:rows])
    stacked = jnp.concatenate(pieces, 0)
    out[...] = lax.dot_general(
        basis[...], stacked, (((1,), (1,)), ((), ())),
        precision=EXACT, preferred_element_type=jnp.float32,
    )


def mode_kernel(count, mixed, times, times_back, rows_in, rows_out, out):
    tm, band, modes, width = mixed.shape
    freqs = times.shape[0] // modes
    length = rows_in.shape[0]
    per = length // band
    slots = width // per

    def dot(a, b):
        return jnp.dot(a, b, precision=EXACT, preferred_element_type=jnp.float32)

    stacked = jnp.concatenate(
        [
            jnp.concatenate(
                [mixed[:, b, :, s * per : (s + 1) * per].reshape(tm * modes, per) for b in range(band)],
                1,
            )
            for s in range(slots)
        ],
        0,
    )
    waves = dot(dot(times[...], stacked), rows_in[...])

    place = lax.axis_index("tm") * band + lax.axis_index("band")
    shape = (modes, length)
    column = place * modes + lax.broadcasted_iota(jnp.int32, shape, 0)
    row = lax.broadcasted_iota(jnp.int32, shape, 1)
    sine_c = jnp.sin(((column + 1) // 2).astype(jnp.float32) * (math.pi / count))
    sine_r = jnp.sin(((row + 1) // 2).astype(jnp.float32) * (math.pi / length))
    depth = sine_c * sine_c + sine_r * sine_r
    top = cheb_t(ORDER, 1.0 - depth * (4.0 / half_width))
    gains = []
    for k in range(freqs):
        if k % 2 == 0:
            lift = cheb_slope * (1.0 - math.cos((k + 1) * math.pi / freqs))
            damp = 1.0 / math.cosh(ORDER * math.acosh((cheb_base + lift) / half_width))
            gain = (1.0 - damp * top) / (4.0 * depth + (cheb_base - 4.0 + lift))
        gains.append(gain)
    waves = waves * jnp.concatenate(gains, 0)

    back = dot(times_back[...], dot(waves, rows_out[...]))
    size = tm * modes
    lane = lax.broadcasted_iota(jnp.int32, (size, LANES), 1)
    for b in range(band):
        rims = back[:size, length + b * LANES : length + (b + 1) * LANES]
        for s in range(slots):
            block = back[s * size : (s + 1) * size]
            out[:, b, :, s * per : (s + 1) * per] = block[:, b * per : (b + 1) * per].reshape(tm, modes, per)
            rims = jnp.where(lane < s * HALO, rims, block[:, length + b * LANES : length + (b + 1) * LANES])
        out[:, b, :, slots * per :] = rims.reshape(tm, modes, LANES)


def force_kernel(phonon, momentum, guess, bonds, edges, after, after_edge, before_ph, after_ph, mixed, basis, sol, mom):
    slices, rows, cols = guess.shape
    parity, tables, expo = setting(phonon, bonds, edges)
    timed = lax.dot_general(
        mixed[...], basis[...], (((0,), (0,)), ((), ())),
        precision=EXACT, preferred_element_type=jnp.float32,
    )
    base = (slices + 1) * rows
    start = [wide(guess[s], edges[s]) for s in range(slices)]
    start.append(last_sign() * wide(after[0], after_edge[0]))
    field = []
    for s in range(slices + 1):
        change = wide(timed[s * rows : (s + 1) * rows], timed[base + s * HALO : base + (s + 1) * HALO])
        field.append(start[s] + relaxation * change)
    for s in range(slices):
        applied = apply_pairs(expo[s] * field[s], FORWARD, tables, *parity)
        image = field[s + 1] - applied
        pulled = apply_pairs(image, BACKWARD, tables, *parity)[:rows]
        own = field[s][:rows]
        sol[s] = own
        fermion = -2.0 * coupling * expo[s][:rows] * own * pulled
        left = before_ph[0] if s == 0 else phonon[s - 1]
        right = after_ph[0] if s == slices - 1 else phonon[s + 1]
        boson = stiffness * (2.0 * phonon[s] - left - right) + mass_term * phonon[s]
        mom[s] = momentum[s] - step_size * (boson + fermion)


def call(kernel, outs, *operands):
    vmem = pl.BlockSpec(memory_space=pltpu.VMEM)
    return pl.pallas_call(
        kernel,
        out_shape=outs,
        in_specs=[vmem] * len(operands),
        out_specs=jax.tree.map(lambda _: vmem, outs),
    )(*map(onchip, operands))


def onchip(value):
    return pltpu.with_memory_space_constraint(value, pltpu.VMEM)


def pack_kernel(guess, *refs):
    tops, ends, outs = refs[:3], refs[3:6], refs[6:]
    first, rims, rim = outs
    first[...] = guess[...]
    early = lax.broadcasted_iota(jnp.int32, tops[0].shape, 1) < EDGE
    at = 0
    for top, end in zip(tops, ends):
        both = jnp.where(early, top[...], end[...]).astype(jnp.float32)
        rims[at : at + top.shape[0]] = both
        if at == 0:
            rim[...] = both[:1]
        at += top.shape[0]


def pack(phonon, guess, bonds):
    slices, rows, cols = guess.shape
    fields = (guess, phonon, bonds)
    last = rows // HALO - 1
    whole = lambda shape: pl.BlockSpec(shape, lambda i: (0, 0, 0))
    tops = [whole((v.shape[0], HALO, cols)) for v in fields]
    ends = [pl.BlockSpec((v.shape[0], HALO, cols), lambda i: (0, last, 0)) for v in fields]
    outs = [(1, rows, cols), (2 * slices + 2, HALO, cols), (1, HALO, cols)]
    return pl.pallas_call(
        pack_kernel,
        grid=(1,),
        out_shape=[pltpu.VMEM(o, jnp.float32) for o in outs],
        in_specs=[whole((1, rows, cols))] + tops + ends,
        out_specs=[whole(o) for o in outs],
    )(guess, *fields, *fields)


def shards(phonon, momentum, source, guess, bonds):
    slices, rows, cols = guess.shape
    tm, band = lax.axis_size("tm"), lax.axis_size("band")
    total, length, devices = tm * slices, rows * band, tm * band
    modes = cols // devices
    f32 = functools.partial(np.asarray, dtype=np.float32)

    slot_times = np.concatenate([time_basis(total, slices * np.arange(tm) + s) for s in range(slices + 1)], 1)
    times = f32(np.kron(slot_times, np.eye(modes)))
    rim = np.arange(HALO)
    rim_rows = []
    for b in range(band):
        row = np.where(rim < EDGE, (b + 1) * rows + rim, b * rows + rim - HALO) % length
        rim_rows.append(np.resize(row, LANES))
    rows_in = f32(space_basis(length, np.arange(length)).T)
    rows_out = f32(space_basis(length, np.concatenate([np.arange(length)] + rim_rows)))
    columns = f32(space_basis(cols, np.arange(cols)))

    first, rims, rim = pack(phonon, guess, bonds)
    edges = band_halo(rims, 0)
    after = shifted(first, 1, 0)
    after_edge = band_halo(rim, 1)

    width = (slices + 1) * rows
    sent = call(
        residual_kernel, jax.ShapeDtypeStruct((cols, width), jnp.float32),
        phonon, source, guess, bonds, edges, after, after_edge, columns,
    )
    mixed = lax.all_to_all(sent.reshape(devices, modes, width), AXES, 0, 0, tiled=True)
    after_ph = shifted(phonon[:1], 1, 0)
    before_ph = shifted(phonon[-1:], -1, 0)
    back = call(
        functools.partial(mode_kernel, cols),
        jax.ShapeDtypeStruct((tm, band, modes, width + LANES), jnp.float32),
        mixed.reshape(tm, band, modes, width), times, np.ascontiguousarray(times.T), rows_in, rows_out,
    )
    mixed = lax.all_to_all(back.reshape(devices, modes, width + LANES), AXES, 0, 0, tiled=True)
    like = jax.ShapeDtypeStruct(guess.shape, jnp.float32)
    return call(
        force_kernel, (like, like),
        phonon, momentum, guess, bonds, edges, after, after_edge, before_ph, after_ph,
        mixed.reshape(cols, width + LANES), columns,
    )


def solution(mesh):
    spec = P("tm", "band", None)
    return jax.shard_map(
        shards,
        mesh=mesh,
        in_specs=(spec, spec, spec, spec, P(None, "band", None)),
        out_specs=(spec, spec),
        check_vma=False,
    )
```

```python
import functools
import math

import numpy as np

import jax
import jax.numpy as jnp
from jax import lax
from jax.experimental import pallas as pl
from jax.experimental.pallas import tpu as pltpu
from jax.sharding import PartitionSpec as P

ORDER = 24

hop_angle = 0.3
coupling = 0.2
stiffness = 1.0
mass_term = 0.5
relaxation = 0.25
step_size = 0.25
cheb_base = 4.03
cheb_slope = 0.5
half_width = 4.0

EDGE = 4
HALO = 2 * EDGE
NEAR = 2
RIM = 2 * NEAR
AXES = ("tm", "band")
ROWS_BY_COLS = (((1,), (0,)), ((), ()))
ROWS_BY_ROWS = (((1,), (1,)), ((), ()))


def shifted(value, dt, db):
    tm, band = lax.axis_size("tm"), lax.axis_size("band")
    pairs = [
        (((t + dt) % tm) * band + (b + db) % band, t * band + b)
        for t in range(tm)
        for b in range(band)
    ]
    return lax.ppermute(value, AXES, pairs)


def band_halo(tile, dt):
    if lax.axis_size("band") == 2:
        return shifted(tile, dt, 1)
    after = shifted(tile[..., :EDGE, :], dt, 1)
    before = shifted(tile[..., EDGE:, :], dt, -1)
    return jnp.concatenate([after, before], -2)


def time_basis(slices, at):
    k = np.arange(slices)[:, None]
    phase = (2 * (k // 2) + 1) * np.asarray(at)[None, :] % (2 * slices)
    angle = phase * (math.pi / slices)
    return math.sqrt(2.0 / slices) * np.where(k % 2 == 0, np.cos(angle), np.sin(angle))


def space_basis(length, at):
    mode = np.arange(length)[:, None]
    freq = (mode + 1) // 2
    angle = (freq * np.asarray(at)[None, :] % length) * (2.0 * math.pi / length)
    wave = np.where((mode % 2 == 0) & (mode > 0), np.sin(angle), np.cos(angle))
    norm = np.where((mode == 0) | (2 * freq == length), 1.0, 2.0)
    return np.sqrt(norm / length) * wave


def cheb_t(order, x):
    if order == 0:
        return jnp.ones_like(x)
    if order == 1:
        return x
    if order % 2 == 0:
        half = cheb_t(order // 2, x)
        return 2.0 * half * half - 1.0
    return 2.0 * cheb_t((order + 1) // 2, x) * cheb_t(order // 2, x) - x


def parities(shape):
    row = lax.broadcasted_iota(jnp.int32, shape, 0) % 2 == 0
    col = lax.broadcasted_iota(jnp.int32, shape, 1) % 2 == 0
    return row, col


def turned(value, by, axis):
    return pltpu.roll(value, by % value.shape[axis], axis)


def pair_table(strengths, colour, row_even, col_even):
    axis = 1 if colour < 2 else 0
    even = col_even if colour < 2 else row_even
    here, before = strengths[1 - axis], turned(strengths[1 - axis], 1, axis)
    bond = jnp.where(even, here, before) if colour % 2 == 0 else jnp.where(even, before, here)
    return 1.0 + (math.cosh(hop_angle) - 1.0) * bond, math.sinh(hop_angle) * bond


def apply_pairs(vector, colours, tables, row_even, col_even):
    for colour in colours:
        axis = 1 if colour < 2 else 0
        even = col_even if colour < 2 else row_even
        ahead, behind = turned(vector, -1, axis), turned(vector, 1, axis)
        first, second = (ahead, behind) if colour % 2 == 0 else (behind, ahead)
        cosh_part, sinh_part = tables[colour]
        vector = cosh_part * vector + sinh_part * jnp.where(even, first, second)
    return vector


def last_sign():
    at_end = lax.axis_index("tm") == lax.axis_size("tm") - 1
    return jnp.where(at_end, -1.0, 1.0).astype(jnp.float32)


def halves(value):
    high = value.astype(jnp.bfloat16)
    return high, (value - high.astype(jnp.float32)).astype(jnp.bfloat16)


def const_halves(value):
    high = np.asarray(value, np.float32).astype(jnp.bfloat16)
    low = (value - high.astype(np.float64)).astype(np.float32).astype(jnp.bfloat16)
    return np.stack([high, low])


def product(a, b, dims=ROWS_BY_COLS):
    dot = functools.partial(lax.dot_general, dimension_numbers=dims, preferred_element_type=jnp.float32)
    return dot(a[0], b[0]) + (dot(a[0], b[1]) + dot(a[1], b[0]))


def wide(main, halo):
    return jnp.concatenate([main, halo], 0)


def local_kernel(phonon, guess, bonds, expo, tables, inner):
    slices, rows, cols = guess.shape
    parity = parities((rows, cols))
    strengths = (bonds[0].astype(jnp.float32), bonds[1].astype(jnp.float32))
    pairs = [pair_table(strengths, q, *parity) for q in range(3)]
    for q in range(3):
        for part in range(2):
            tables[2 * q + part] = pairs[q][part]
    for s in range(slices):
        expo[s] = jnp.exp(-coupling * phonon[s])
        inner[s] = apply_pairs(expo[s] * guess[s], (0, 1, 2), pairs, *parity)


class Band:
    def __init__(self, bonds, edges, expo, tables, slices):
        _, rows, cols = bonds.shape
        self.rows, self.slices = rows, slices
        self.main, self.strip, self.all = (parities((n, cols)) for n in (rows, HALO, rows + HALO))
        across, down = edges[2 * slices], edges[2 * slices + 1]
        self.pairs = [(tables[2 * q], tables[2 * q + 1]) for q in range(3)]
        self.strip_pairs = [pair_table((across, down), q, *self.strip) for q in range(3)]
        vertical = wide(bonds[1].astype(jnp.float32), down)
        self.wide_pairs = {3: pair_table((None, vertical), 3, *self.all)}
        self.expo = [expo[s] for s in range(slices)]
        self.strip_expo = [jnp.exp(-coupling * edges[slices + s]) for s in range(slices)]

    def inner(self, s, field):
        return apply_pairs(self.expo[s] * field, (0, 1, 2), self.pairs, *self.main)

    def propagated(self, s, inner, strip):
        strip = apply_pairs(self.strip_expo[s] * strip, (0, 1, 2), self.strip_pairs, *self.strip)
        return apply_pairs(wide(inner, strip), (3,), self.wide_pairs, *self.all)

    def pulled(self, field):
        field = apply_pairs(field, (3,), self.wide_pairs, *self.all)[: self.rows]
        return apply_pairs(field, (2, 1, 0), self.pairs, *self.main)


def residual_kernel(source, guess, bonds, edges, after, after_edge, expo, tables, inner, basis, out):
    slices, rows, cols = guess.shape
    band = Band(bonds, edges, expo, tables, slices)
    field = [wide(guess[s], edges[s]) for s in range(slices)]
    field.append(last_sign() * wide(after[0], after_edge[0]))
    pieces = []
    link = field[0]
    for s in range(slices):
        applied = band.propagated(s, inner[s], edges[s])
        following = field[s + 1] - applied
        pieces.append(source[s] - link[:rows] + band.expo[s] * band.pulled(following))
        link = following
    pieces.append(applied[:rows])
    stacked = jnp.concatenate(pieces, 0)
    out[...] = product(basis, halves(stacked), ROWS_BY_ROWS)


def mode_kernel(count, mixed, times, times_back, rows_in, rims, out):
    tm, band, modes, width = mixed.shape
    size = tm * modes
    freqs = times.shape[1] // modes
    length = rows_in.shape[1]
    per = length // band
    slots = width // per
    chunk = slots * modes + 1

    stacked = jnp.concatenate(
        [
            jnp.concatenate(
                [mixed[:, b, :, s * per : (s + 1) * per].reshape(size, per) for b in range(band)], 1
            )
            for s in range(slots)
        ],
        0,
    )
    waves = product(halves(product(times, halves(stacked))), rows_in)

    place = lax.axis_index("tm") * band + lax.axis_index("band")
    shape = (modes, length)
    column = place * modes + lax.broadcasted_iota(jnp.int32, shape, 0)
    row = lax.broadcasted_iota(jnp.int32, shape, 1)
    sine_c = jnp.sin(((column + 1) // 2).astype(jnp.float32) * (math.pi / count))
    sine_r = jnp.sin(((row + 1) // 2).astype(jnp.float32) * (math.pi / length))
    depth = sine_c * sine_c + sine_r * sine_r
    top = cheb_t(ORDER, 1.0 - depth * (4.0 / half_width))
    gains = []
    for k in range(freqs):
        if k % 2 == 0:
            lift = cheb_slope * (1.0 - math.cos((k + 1) * math.pi / freqs))
            damp = 1.0 / math.cosh(ORDER * math.acosh((cheb_base + lift) / half_width))
            gain = (1.0 - damp * top) / (4.0 * depth + (cheb_base - 4.0 + lift))
        gains.append(gain)
    waves = halves(waves * jnp.concatenate(gains, 0))

    back = product(times_back, halves(product(waves, rows_in, ROWS_BY_ROWS)))
    edge = product(halves(product(halves(rims[...]), waves, ROWS_BY_ROWS)), times)
    turns = [
        pltpu.roll(edge[:, s * size : (s + 1) * size], RIM * s * modes, 1, stride=modes, stride_axis=0)
        for s in range(slots)
    ]
    group = lax.broadcasted_iota(jnp.int32, (tm, size), 1) // modes
    slot = group - lax.broadcasted_iota(jnp.int32, (tm, size), 0)
    slot = jnp.where(slot < 0, slot + tm, slot)
    for b in range(band):
        rim = jnp.zeros((tm, size), jnp.float32)
        for s in range(slots):
            for q in range(RIM):
                line = turns[s][b * RIM + q : b * RIM + q + 1]
                rim = jnp.where(slot == (RIM * (s + b) + q) % tm, line, rim)
        for p in range(tm):
            at = (p * band + b) * chunk
            for s in range(slots):
                start = s * size + p * modes
                out[at + s * modes : at + (s + 1) * modes] = back[start : start + modes, b * per : (b + 1) * per]
            out[at + slots * modes : at + chunk] = rim[p : p + 1]


def force_kernel(base, guess, bonds, edges, after, after_edge, expo, tables, mixed, basis, sol, mom, turned_edge):
    slices, rows, cols = guess.shape
    devices = lax.axis_size("tm") * lax.axis_size("band")
    modes = cols // devices
    slots = slices + 1
    chunk = slots * modes + 1
    band = Band(bonds, edges, expo, tables, slices)
    columns = (basis[0], basis[1])

    arrived = [
        jnp.concatenate([mixed[d * chunk + s * modes : d * chunk + (s + 1) * modes] for d in range(devices)], 0)
        for s in range(slots)
    ]
    timed = product(halves(jnp.concatenate(arrived, 1).T), columns)

    rim = mixed[pl.ds(slots * modes, devices, stride=chunk), :]
    lanes = rim.shape[1]
    by = modes * (lax.axis_index("tm") + RIM * lax.axis_index("band"))
    rim = pltpu.roll(rim, lax.rem(2 * lanes - by, lanes), 1)
    turned_edge[...] = rim.T
    groups = lanes // modes
    lines = jnp.concatenate([turned_edge[pl.ds(m, groups, stride=modes), :] for m in range(modes)], 1)
    order = jnp.concatenate(
        [jnp.concatenate([part.reshape(devices, modes, cols)[:, m] for m in range(modes)], 0)[None] for part in columns], 0
    )
    strips = product(halves(lines), order)

    start = [wide(guess[s], edges[s]) for s in range(slices)]
    start.append(last_sign() * wide(after[0], after_edge[0]))
    field = []
    for s in range(slots):
        strip = turned(strips[s * RIM : s * RIM + HALO], -NEAR, 0)
        field.append(start[s] + relaxation * wide(timed[s * rows : (s + 1) * rows], strip))
    for s in range(slices):
        own = field[s][:rows]
        image = field[s + 1] - band.propagated(s, band.inner(s, own), field[s][rows:])
        sol[s] = own
        fermion = -2.0 * coupling * band.expo[s] * own * band.pulled(image)
        mom[s] = base[s] - step_size * fermion


def call(kernel, outs, *operands, flops=0, **kwargs):
    vmem = pl.BlockSpec(memory_space=pltpu.VMEM)
    return pl.pallas_call(
        kernel,
        out_shape=outs,
        in_specs=[vmem] * len(operands),
        out_specs=jax.tree.map(lambda _: vmem, outs),
        cost_estimate=pl.CostEstimate(flops=flops, bytes_accessed=4 << 20, transcendentals=0),
        **kwargs,
    )(*map(onchip, operands))


def onchip(value):
    return pltpu.with_memory_space_constraint(value, pltpu.VMEM)


def pack_kernel(guess, *refs):
    tops, ends, outs = refs[:3], refs[3:6], refs[6:]
    first, rims, rim = outs
    first[...] = guess[...]
    early = lax.broadcasted_iota(jnp.int32, tops[0].shape, 1) < EDGE
    at = 0
    for top, end in zip(tops, ends):
        both = jnp.where(early, top[...], end[...]).astype(jnp.float32)
        rims[at : at + top.shape[0]] = both
        if at == 0:
            rim[...] = both[:1]
        at += top.shape[0]


def pack(phonon, guess, bonds):
    slices, rows, cols = guess.shape
    fields = (guess, phonon, bonds)
    last = rows // HALO - 1
    whole = lambda shape: pl.BlockSpec(shape, lambda i: (0, 0, 0))
    tops = [whole((v.shape[0], HALO, cols)) for v in fields]
    ends = [pl.BlockSpec((v.shape[0], HALO, cols), lambda i: (0, last, 0)) for v in fields]
    outs = [(1, rows, cols), (2 * slices + 2, HALO, cols), (1, HALO, cols)]
    return pl.pallas_call(
        pack_kernel,
        grid=(1,),
        out_shape=[pltpu.VMEM(o, jnp.float32) for o in outs],
        in_specs=[whole((1, rows, cols))] + tops + ends,
        out_specs=[whole(o) for o in outs],
    )(guess, *fields, *fields)


def shards(phonon, momentum, source, guess, bonds):
    slices, rows, cols = guess.shape
    tm, band = lax.axis_size("tm"), lax.axis_size("band")
    total, length, devices = tm * slices, rows * band, tm * band
    modes = cols // devices
    slots = slices + 1

    slot_times = np.concatenate([time_basis(total, slices * np.arange(tm) + s) for s in range(slots)], 1)
    times = np.kron(slot_times, np.eye(modes))
    near = np.concatenate([np.arange(-NEAR, 0), rows + np.arange(NEAR)])
    rim_sites = np.concatenate([(b * rows + near) % length for b in range(band)])
    rims_basis = np.asarray(space_basis(length, rim_sites).T, np.float32)
    rows_in = const_halves(space_basis(length, np.arange(length)).T)
    columns = const_halves(space_basis(cols, np.arange(cols)))

    first, rims, rim = pack(phonon, guess, bonds)
    edges = band_halo(rims, 0)
    after = shifted(first, 1, 0)
    after_edge = band_halo(rim, 1)

    on = lambda *shape: pltpu.VMEM(shape, jnp.float32)
    expo, tables, inner = call(
        local_kernel, (on(slices, rows, cols), on(6, rows, cols), on(slices, rows, cols)),
        phonon, guess, bonds,
    )
    sent = call(
        residual_kernel, jax.ShapeDtypeStruct((cols, slots * rows), jnp.float32),
        source, guess, bonds, edges, after, after_edge, expo, tables, inner, columns,
    )
    mixed = lax.all_to_all(sent.reshape(devices, modes, slots * rows), AXES, 0, 0, tiled=True)
    wave_rows = devices * (slots * modes + 1)
    back = call(
        functools.partial(mode_kernel, cols), jax.ShapeDtypeStruct((wave_rows, rows), jnp.float32),
        mixed.reshape(tm, band, modes, slots * rows),
        const_halves(times), const_halves(np.ascontiguousarray(times.T)), rows_in, rims_basis,
    )
    mixed = lax.all_to_all(back.reshape(devices, 1, -1), AXES, 0, 0, tiled=True)

    after_ph = shifted(phonon[:1], 1, 0)
    before_ph = shifted(phonon[-1:], -1, 0)
    ring = jnp.concatenate([before_ph, phonon, after_ph], 0)
    boson = stiffness * (2.0 * phonon - ring[:-2] - ring[2:]) + mass_term * phonon
    base = momentum - step_size * boson
    like = jax.ShapeDtypeStruct(guess.shape, jnp.float32)
    return call(
        force_kernel, (like, like),
        base, guess, bonds, edges, after, after_edge, expo, tables,
        mixed.reshape(wave_rows, rows), columns,
        scratch_shapes=[pltpu.VMEM((cols // band, devices), jnp.float32)],
    )


def solution(mesh):
    spec = P("tm", "band", None)
    return jax.shard_map(
        shards,
        mesh=mesh,
        in_specs=(spec, spec, spec, spec, P(None, "band", None)),
        out_specs=(spec, spec),
        check_vma=False,
    )
```

```python
import functools
import math

import numpy as np

import jax
import jax.numpy as jnp
from jax import lax
from jax.experimental import pallas as pl
from jax.experimental.pallas import tpu as pltpu
from jax.sharding import PartitionSpec as P

ORDER = 24

hop_angle = 0.3
coupling = 0.2
stiffness = 1.0
mass_term = 0.5
relaxation = 0.25
step_size = 0.25
cheb_base = 4.03
cheb_slope = 0.5
half_width = 4.0

EDGE = 4
HALO = 2 * EDGE
NEAR = 2
RIM = 2 * NEAR
AXES = ("tm", "band")
ROWS_BY_COLS = (((1,), (0,)), ((), ()))
ROWS_BY_ROWS = (((1,), (1,)), ((), ()))


def shifted(value, dt, db):
    tm, band = lax.axis_size("tm"), lax.axis_size("band")
    pairs = [
        (((t + dt) % tm) * band + (b + db) % band, t * band + b)
        for t in range(tm)
        for b in range(band)
    ]
    return lax.ppermute(value, AXES, pairs)


def band_halo(tile, dt):
    if lax.axis_size("band") == 2:
        return shifted(tile, dt, 1)
    after = shifted(tile[..., :EDGE, :], dt, 1)
    before = shifted(tile[..., EDGE:, :], dt, -1)
    return jnp.concatenate([after, before], -2)


def time_basis(slices, at):
    k = np.arange(slices)[:, None]
    phase = (2 * (k // 2) + 1) * np.asarray(at)[None, :] % (2 * slices)
    angle = phase * (math.pi / slices)
    return math.sqrt(2.0 / slices) * np.where(k % 2 == 0, np.cos(angle), np.sin(angle))


def space_basis(length, at):
    mode = np.arange(length)[:, None]
    freq = (mode + 1) // 2
    angle = (freq * np.asarray(at)[None, :] % length) * (2.0 * math.pi / length)
    wave = np.where((mode % 2 == 0) & (mode > 0), np.sin(angle), np.cos(angle))
    norm = np.where((mode == 0) | (2 * freq == length), 1.0, 2.0)
    return np.sqrt(norm / length) * wave


def cheb_t(order, x):
    if order == 0:
        return jnp.ones_like(x)
    if order == 1:
        return x
    if order % 2 == 0:
        half = cheb_t(order // 2, x)
        return 2.0 * half * half - 1.0
    return 2.0 * cheb_t((order + 1) // 2, x) * cheb_t(order // 2, x) - x


def parities(shape):
    row = lax.broadcasted_iota(jnp.int32, shape, 0) % 2 == 0
    col = lax.broadcasted_iota(jnp.int32, shape, 1) % 2 == 0
    return row, col


def turned(value, by, axis):
    return pltpu.roll(value, by % value.shape[axis], axis)


def pair_table(strengths, colour, row_even, col_even):
    axis = 1 if colour < 2 else 0
    even = col_even if colour < 2 else row_even
    here, before = strengths[1 - axis], turned(strengths[1 - axis], 1, axis)
    bond = jnp.where(even, here, before) if colour % 2 == 0 else jnp.where(even, before, here)
    return 1.0 + (math.cosh(hop_angle) - 1.0) * bond, math.sinh(hop_angle) * bond


def apply_pairs(vector, colours, tables, row_even, col_even):
    for colour in colours:
        axis = 1 if colour < 2 else 0
        even = col_even if colour < 2 else row_even
        ahead, behind = turned(vector, -1, axis), turned(vector, 1, axis)
        first, second = (ahead, behind) if colour % 2 == 0 else (behind, ahead)
        cosh_part, sinh_part = tables[colour]
        vector = cosh_part * vector + sinh_part * jnp.where(even, first, second)
    return vector


def last_sign():
    at_end = lax.axis_index("tm") == lax.axis_size("tm") - 1
    return jnp.where(at_end, -1.0, 1.0).astype(jnp.float32)


def halves(value):
    high = value.astype(jnp.bfloat16)
    return high, (value - high.astype(jnp.float32)).astype(jnp.bfloat16)


def const_halves(value):
    high = np.asarray(value, np.float32).astype(jnp.bfloat16)
    low = (value - high.astype(np.float64)).astype(np.float32).astype(jnp.bfloat16)
    return np.stack([high, low])


def product(a, b, dims=ROWS_BY_COLS):
    dot = functools.partial(lax.dot_general, dimension_numbers=dims, preferred_element_type=jnp.float32)
    return dot(a[0], b[0]) + (dot(a[0], b[1]) + dot(a[1], b[0]))


def wide(main, halo):
    return jnp.concatenate([main, halo], 0)


def local_kernel(phonon, guess, bonds, expo, tables, inner):
    slices, rows, cols = guess.shape
    parity = parities((rows, cols))
    strengths = (bonds[0].astype(jnp.float32), bonds[1].astype(jnp.float32))
    pairs = [pair_table(strengths, q, *parity) for q in range(3)]
    for q in range(3):
        for part in range(2):
            tables[2 * q + part] = pairs[q][part]
    for s in range(slices):
        expo[s] = jnp.exp(-coupling * phonon[s])
        inner[s] = apply_pairs(expo[s] * guess[s], (0, 1, 2), pairs, *parity)


class Band:
    def __init__(self, bonds, edges, expo, tables, slices):
        _, rows, cols = bonds.shape
        self.rows, self.slices = rows, slices
        self.main, self.strip, self.all = (parities((n, cols)) for n in (rows, HALO, rows + HALO))
        across, down = edges[2 * slices], edges[2 * slices + 1]
        self.pairs = [(tables[2 * q], tables[2 * q + 1]) for q in range(3)]
        self.strip_pairs = [pair_table((across, down), q, *self.strip) for q in range(3)]
        vertical = wide(bonds[1].astype(jnp.float32), down)
        self.wide_pairs = {3: pair_table((None, vertical), 3, *self.all)}
        self.expo = [expo[s] for s in range(slices)]
        self.strip_expo = [jnp.exp(-coupling * edges[slices + s]) for s in range(slices)]

    def inner(self, s, field):
        return apply_pairs(self.expo[s] * field, (0, 1, 2), self.pairs, *self.main)

    def propagated(self, s, inner, strip):
        strip = apply_pairs(self.strip_expo[s] * strip, (0, 1, 2), self.strip_pairs, *self.strip)
        return apply_pairs(wide(inner, strip), (3,), self.wide_pairs, *self.all)

    def pulled(self, field):
        field = apply_pairs(field, (3,), self.wide_pairs, *self.all)[: self.rows]
        return apply_pairs(field, (2, 1, 0), self.pairs, *self.main)


def residual_kernel(source, guess, bonds, edges, after, after_edge, expo, tables, inner, basis, out):
    slices, rows, cols = guess.shape
    band = Band(bonds, edges, expo, tables, slices)
    field = [wide(guess[s], edges[s]) for s in range(slices)]
    field.append(last_sign() * wide(after[0], after_edge[0]))
    pieces = []
    link = field[0]
    for s in range(slices):
        applied = band.propagated(s, inner[s], edges[s])
        following = field[s + 1] - applied
        pieces.append(source[s] - link[:rows] + band.expo[s] * band.pulled(following))
        link = following
    pieces.append(applied[:rows])
    stacked = jnp.concatenate(pieces, 0)
    out[...] = product(basis, halves(stacked), ROWS_BY_ROWS)


def mode_kernel(count, mixed, times, times_back, rows_in, rims, out):
    tm, band, modes, width = mixed.shape
    size = tm * modes
    freqs = times.shape[1] // modes
    length = rows_in.shape[1]
    per = length // band
    slots = width // per
    chunk = slots * modes + 1

    stacked = jnp.concatenate(
        [
            jnp.concatenate(
                [mixed[:, b, :, s * per : (s + 1) * per].reshape(size, per) for b in range(band)], 1
            )
            for s in range(slots)
        ],
        0,
    )
    waves = product(halves(product(times, halves(stacked))), rows_in)

    place = lax.axis_index("tm") * band + lax.axis_index("band")
    shape = (modes, length)
    column = place * modes + lax.broadcasted_iota(jnp.int32, shape, 0)
    row = lax.broadcasted_iota(jnp.int32, shape, 1)
    sine_c = jnp.sin(((column + 1) // 2).astype(jnp.float32) * (math.pi / count))
    sine_r = jnp.sin(((row + 1) // 2).astype(jnp.float32) * (math.pi / length))
    depth = sine_c * sine_c + sine_r * sine_r
    top = cheb_t(ORDER, 1.0 - depth * (4.0 / half_width))
    gains = []
    for k in range(freqs):
        if k % 2 == 0:
            lift = cheb_slope * (1.0 - math.cos((k + 1) * math.pi / freqs))
            damp = 1.0 / math.cosh(ORDER * math.acosh((cheb_base + lift) / half_width))
            gain = (1.0 - damp * top) / (4.0 * depth + (cheb_base - 4.0 + lift))
        gains.append(gain)
    waves = halves(waves * jnp.concatenate(gains, 0))

    back = product(times_back, halves(product(waves, rows_in, ROWS_BY_ROWS)))
    edge = product(halves(product(halves(rims[...]), waves, ROWS_BY_ROWS)), times)
    turns = [
        pltpu.roll(edge[:, s * size : (s + 1) * size], RIM * s * modes, 1, stride=modes, stride_axis=0)
        for s in range(slots)
    ]
    group = lax.broadcasted_iota(jnp.int32, (tm, size), 1) // modes
    slot = group - lax.broadcasted_iota(jnp.int32, (tm, size), 0)
    slot = jnp.where(slot < 0, slot + tm, slot)
    for b in range(band):
        rim = jnp.zeros((tm, size), jnp.float32)
        for s in range(slots):
            for q in range(RIM):
                line = turns[s][b * RIM + q : b * RIM + q + 1]
                rim = jnp.where(slot == (RIM * (s + b) + q) % tm, line, rim)
        for p in range(tm):
            at = (p * band + b) * chunk
            for s in range(slots):
                start = s * size + p * modes
                out[at + s * modes : at + (s + 1) * modes] = back[start : start + modes, b * per : (b + 1) * per]
            out[at + slots * modes : at + chunk] = rim[p : p + 1]


def force_kernel(base, guess, bonds, edges, after, after_edge, expo, tables, mixed, basis, sol, mom, turned_edge):
    slices, rows, cols = guess.shape
    devices = lax.axis_size("tm") * lax.axis_size("band")
    modes = cols // devices
    slots = slices + 1
    chunk = slots * modes + 1
    band = Band(bonds, edges, expo, tables, slices)
    columns = (basis[0], basis[1])

    arrived = [
        jnp.concatenate([mixed[d * chunk + s * modes : d * chunk + (s + 1) * modes] for d in range(devices)], 0)
        for s in range(slots)
    ]
    timed = product(halves(jnp.concatenate(arrived, 1).T), columns)

    rim = mixed[pl.ds(slots * modes, devices, stride=chunk), :]
    lanes = rim.shape[1]
    by = modes * (lax.axis_index("tm") + RIM * lax.axis_index("band"))
    rim = pltpu.roll(rim, lax.rem(2 * lanes - by, lanes), 1)
    turned_edge[...] = rim.T
    groups = lanes // modes
    lines = jnp.concatenate([turned_edge[pl.ds(m, groups, stride=modes), :] for m in range(modes)], 1)
    order = jnp.concatenate(
        [jnp.concatenate([part.reshape(devices, modes, cols)[:, m] for m in range(modes)], 0)[None] for part in columns], 0
    )
    strips = product(halves(lines), order)

    start = [wide(guess[s], edges[s]) for s in range(slices)]
    start.append(last_sign() * wide(after[0], after_edge[0]))
    field = []
    for s in range(slots):
        strip = turned(strips[s * RIM : s * RIM + HALO], -NEAR, 0)
        field.append(start[s] + relaxation * wide(timed[s * rows : (s + 1) * rows], strip))
    for s in range(slices):
        own = field[s][:rows]
        image = field[s + 1] - band.propagated(s, band.inner(s, own), field[s][rows:])
        sol[s] = own
        fermion = -2.0 * coupling * band.expo[s] * own * band.pulled(image)
        mom[s] = base[s] - step_size * fermion


def call(kernel, outs, *operands, flops=0, **kwargs):
    vmem = pl.BlockSpec(memory_space=pltpu.VMEM)
    return pl.pallas_call(
        kernel,
        out_shape=outs,
        in_specs=[vmem] * len(operands),
        out_specs=jax.tree.map(lambda _: vmem, outs),
        compiler_params=pltpu.CompilerParams(vmem_limit_bytes=12 << 20),
        cost_estimate=pl.CostEstimate(flops=flops, bytes_accessed=4 << 20, transcendentals=0),
        **kwargs,
    )(*map(onchip, operands))


def onchip(value):
    return pltpu.with_memory_space_constraint(value, pltpu.VMEM)


def pack_kernel(guess, *refs):
    tops, ends, outs = refs[:3], refs[3:6], refs[6:]
    first, rims, rim = outs
    first[...] = guess[...]
    early = lax.broadcasted_iota(jnp.int32, tops[0].shape, 1) < EDGE
    at = 0
    for top, end in zip(tops, ends):
        both = jnp.where(early, top[...], end[...]).astype(jnp.float32)
        rims[at : at + top.shape[0]] = both
        if at == 0:
            rim[...] = both[:1]
        at += top.shape[0]


def pack(phonon, guess, bonds):
    slices, rows, cols = guess.shape
    fields = (guess, phonon, bonds)
    last = rows // HALO - 1
    whole = lambda shape: pl.BlockSpec(shape, lambda i: (0, 0, 0))
    tops = [whole((v.shape[0], HALO, cols)) for v in fields]
    ends = [pl.BlockSpec((v.shape[0], HALO, cols), lambda i: (0, last, 0)) for v in fields]
    outs = [(1, rows, cols), (2 * slices + 2, HALO, cols), (1, HALO, cols)]
    return pl.pallas_call(
        pack_kernel,
        grid=(1,),
        out_shape=[pltpu.VMEM(o, jnp.float32) for o in outs],
        in_specs=[whole((1, rows, cols))] + tops + ends,
        out_specs=[whole(o) for o in outs],
    )(guess, *fields, *fields)


def shards(phonon, momentum, source, guess, bonds):
    slices, rows, cols = guess.shape
    tm, band = lax.axis_size("tm"), lax.axis_size("band")
    total, length, devices = tm * slices, rows * band, tm * band
    modes = cols // devices
    slots = slices + 1

    slot_times = np.concatenate([time_basis(total, slices * np.arange(tm) + s) for s in range(slots)], 1)
    times = np.kron(slot_times, np.eye(modes))
    near = np.concatenate([np.arange(-NEAR, 0), rows + np.arange(NEAR)])
    rim_sites = np.concatenate([(b * rows + near) % length for b in range(band)])
    rims_basis = np.asarray(space_basis(length, rim_sites).T, np.float32)
    rows_in = const_halves(space_basis(length, np.arange(length)).T)
    columns = const_halves(space_basis(cols, np.arange(cols)))

    first, rims, rim = pack(phonon, guess, bonds)
    edges = band_halo(rims, 0)
    after = shifted(first, 1, 0)
    after_edge = band_halo(rim, 1)

    on = lambda *shape: pltpu.VMEM(shape, jnp.float32)
    expo, tables, inner = call(
        local_kernel, (on(slices, rows, cols), on(6, rows, cols), on(slices, rows, cols)),
        phonon, guess, bonds,
    )
    sent = call(
        residual_kernel, jax.ShapeDtypeStruct((cols, slots * rows), jnp.float32),
        source, guess, bonds, edges, after, after_edge, expo, tables, inner, columns,
    )
    mixed = lax.all_to_all(sent.reshape(devices, modes, slots * rows), AXES, 0, 0, tiled=True)
    wave_rows = devices * (slots * modes + 1)
    back = call(
        functools.partial(mode_kernel, cols), jax.ShapeDtypeStruct((wave_rows, rows), jnp.float32),
        mixed.reshape(tm, band, modes, slots * rows),
        const_halves(times), const_halves(np.ascontiguousarray(times.T)), rows_in, rims_basis,
    )
    mixed = lax.all_to_all(back.reshape(devices, 1, -1), AXES, 0, 0, tiled=True)

    after_ph = shifted(phonon[:1], 1, 0)
    before_ph = shifted(phonon[-1:], -1, 0)
    ring = jnp.concatenate([before_ph, phonon, after_ph], 0)
    boson = stiffness * (2.0 * phonon - ring[:-2] - ring[2:]) + mass_term * phonon
    base = momentum - step_size * boson
    like = jax.ShapeDtypeStruct(guess.shape, jnp.float32)
    return call(
        force_kernel, (like, like),
        base, guess, bonds, edges, after, after_edge, expo, tables,
        mixed.reshape(wave_rows, rows), columns,
        scratch_shapes=[pltpu.VMEM((cols // band, devices), jnp.float32)],
    )


def solution(mesh):
    spec = P("tm", "band", None)
    return jax.shard_map(
        shards,
        mesh=mesh,
        in_specs=(spec, spec, spec, spec, P(None, "band", None)),
        out_specs=(spec, spec),
        check_vma=False,
    )
```

```python
import functools
import math

import numpy as np

import jax
import jax.numpy as jnp
from jax import lax
from jax.experimental import pallas as pl
from jax.experimental.pallas import tpu as pltpu
from jax.sharding import PartitionSpec as P


ORDER = 24

hop_angle = 0.3
coupling = 0.2
stiffness = 1.0
mass_term = 0.5
relaxation = 0.25
step_size = 0.25
cheb_base = 4.03
cheb_slope = 0.5
half_width = 4.0

EDGE = 4
HALO = 2 * EDGE
SUBLANES = 8
LANES = 128
NEAR = 2
RIM = 2 * NEAR
AXES = ("tm", "band")
ROWS_BY_COLS = (((1,), (0,)), ((), ()))
ROWS_BY_ROWS = (((1,), (1,)), ((), ()))


def shifted(value, dt, db):
    tm, band = lax.axis_size("tm"), lax.axis_size("band")
    pairs = [
        (((t + dt) % tm) * band + (b + db) % band, t * band + b)
        for t in range(tm)
        for b in range(band)
    ]
    return lax.ppermute(value, AXES, pairs)


def band_halo(tile, dt):
    if lax.axis_size("band") == 2:
        return shifted(tile, dt, 1)
    after = shifted(tile[..., :EDGE, :], dt, 1)
    before = shifted(tile[..., EDGE:, :], dt, -1)
    return jnp.concatenate([after, before], -2)


def time_basis(slices, at):
    k = np.arange(slices)[:, None]
    phase = (2 * (k // 2) + 1) * np.asarray(at)[None, :] % (2 * slices)
    angle = phase * (math.pi / slices)
    return math.sqrt(2.0 / slices) * np.where(k % 2 == 0, np.cos(angle), np.sin(angle))


def space_basis(length, at):
    mode = np.arange(length)[:, None]
    freq = (mode + 1) // 2
    angle = (freq * np.asarray(at)[None, :] % length) * (2.0 * math.pi / length)
    wave = np.where((mode % 2 == 0) & (mode > 0), np.sin(angle), np.cos(angle))
    norm = np.where((mode == 0) | (2 * freq == length), 1.0, 2.0)
    return np.sqrt(norm / length) * wave


def cheb_t(order, x):
    if order == 0:
        return jnp.ones_like(x)
    if order == 1:
        return x
    if order % 2 == 0:
        half = cheb_t(order // 2, x)
        return 2.0 * half * half - 1.0
    return 2.0 * cheb_t((order + 1) // 2, x) * cheb_t(order // 2, x) - x


def blocks(value):
    rows, cols = value.shape
    return [value[:, i : i + LANES].reshape(rows // SUBLANES, SUBLANES, LANES) for i in range(0, cols, LANES)]


def joined(parts):
    return jnp.concatenate([part.reshape(-1, LANES) for part in parts], 1)


def each(function, *lists):
    return [function(*items) for items in zip(*lists)]


def taken(part, index):
    numbers = lax.GatherDimensionNumbers(
        offset_dims=(),
        collapsed_slice_dims=(2,),
        start_index_map=(2,),
        operand_batching_dims=(0, 1),
        start_indices_batching_dims=(0, 1),
    )
    return lax.gather(
        part, index[..., None], numbers, (1, 1, 1), mode=lax.GatherScatterMode.PROMISE_IN_BOUNDS
    )


def along_columns(parts, colour):
    place = lax.broadcasted_iota(jnp.int32, parts[0].shape, 2)
    if colour == 0:
        return each(lambda part: taken(part, place ^ 1), parts)
    before, after = parts[-1:] + parts[:-1], parts[1:] + parts[:1]
    if len(parts) == 2:
        outer = (place == 0) | (place == LANES - 1)
        parts = each(lambda mine, other: jnp.where(outer, other, mine), parts, after)
    else:
        parts = each(
            lambda mine, low, high: jnp.where(place == LANES - 1, low, jnp.where(place == 0, high, mine)),
            parts, before, after,
        )
    index = ((((place + LANES - 1) & (LANES - 1)) ^ 1) + 1) & (LANES - 1)
    return each(lambda part: taken(part, index), parts)


def along_rows(parts, colour):
    place = lax.broadcasted_iota(jnp.int32, parts[0].shape, 1)
    even = (place & 1) == 0

    def partner(part):
        up, down = pltpu.roll(part, SUBLANES - 1, 1), pltpu.roll(part, 1, 1)
        if colour == 2:
            return jnp.where(even, up, down)
        inside = jnp.where(even, down, up)
        if part.shape[0] == 1:
            return inside
        low = jnp.concatenate([down[-1:], down[:-1]], 0)
        high = jnp.concatenate([up[1:], up[:1]], 0)
        return jnp.where(place == 0, low, jnp.where(place == SUBLANES - 1, high, inside))

    return each(partner, parts)


def partners(parts, colour):
    return along_columns(parts, colour) if colour < 2 else along_rows(parts, colour)


def pair_table(strengths, colour):
    parts = strengths[colour // 2]
    odd = lax.broadcasted_iota(jnp.int32, parts[0].shape, 2 if colour < 2 else 1) & 1
    holder = odd == colour % 2
    bonds = each(lambda mine, other: jnp.where(holder, mine, other), parts, partners(parts, colour))
    cosh_part = each(lambda bond: 1.0 + (math.cosh(hop_angle) - 1.0) * bond, bonds)
    return cosh_part, each(lambda bond: math.sinh(hop_angle) * bond, bonds)


def apply_pairs(parts, colours, tables):
    for colour in colours:
        mix = lambda mine, other, cosh_part, sinh_part: cosh_part * mine + sinh_part * other
        parts = each(mix, parts, partners(parts, colour), *tables[colour])
    return parts


def last_sign():
    at_end = lax.axis_index("tm") == lax.axis_size("tm") - 1
    return jnp.where(at_end, -1.0, 1.0).astype(jnp.float32)


def halves(value):
    high = value.astype(jnp.bfloat16)
    return high, (value - high.astype(jnp.float32)).astype(jnp.bfloat16)


def const_halves(value):
    high = np.asarray(value, np.float32).astype(jnp.bfloat16)
    low = (value - high.astype(np.float64)).astype(np.float32).astype(jnp.bfloat16)
    return np.stack([high, low])


def product(a, b, dims=ROWS_BY_COLS):
    dot = functools.partial(lax.dot_general, dimension_numbers=dims, preferred_element_type=jnp.float32)
    return dot(a[0], b[0]) + (dot(a[0], b[1]) + dot(a[1], b[0]))


def times(a, b):
    return each(lax.mul, a, b)


def wide(main, halo):
    return each(lambda rows, rim: jnp.concatenate([rows, rim], 0), main, halo)


def local_kernel(phonon, guess, bonds, expo, tables, inner):
    slices = guess.shape[0]
    strengths = [blocks(bonds[d].astype(jnp.float32)) for d in range(2)]
    pairs = [pair_table(strengths, q) for q in range(3)]
    for q in range(3):
        for part in range(2):
            tables[2 * q + part] = joined(pairs[q][part])
    for s in range(slices):
        grown = jnp.exp(-coupling * phonon[s])
        expo[s] = grown
        inner[s] = joined(apply_pairs(blocks(grown * guess[s]), (0, 1, 2), pairs))


class Band:
    def __init__(self, bonds, edges, expo, tables, slices):
        self.tiles = bonds.shape[1] // SUBLANES
        across, down = blocks(edges[2 * slices]), blocks(edges[2 * slices + 1])
        self.pairs = [[blocks(tables[2 * q + part]) for part in range(2)] for q in range(3)]
        self.strip_pairs = [pair_table((across, down), q) for q in range(3)]
        vertical = wide(blocks(bonds[1].astype(jnp.float32)), down)
        self.wide_pairs = {3: pair_table((None, vertical), 3)}
        self.expo = [blocks(expo[s]) for s in range(slices)]
        self.strip_expo = [blocks(jnp.exp(-coupling * edges[slices + s])) for s in range(slices)]

    def own(self, parts):
        return each(lambda part: part[: self.tiles], parts)

    def rim(self, parts):
        return each(lambda part: part[self.tiles :], parts)

    def inner(self, s, field):
        return apply_pairs(times(self.expo[s], field), (0, 1, 2), self.pairs)

    def propagated(self, s, inner, strip):
        strip = apply_pairs(times(self.strip_expo[s], strip), (0, 1, 2), self.strip_pairs)
        return apply_pairs(wide(inner, strip), (3,), self.wide_pairs)

    def pulled(self, field):
        field = self.own(apply_pairs(field, (3,), self.wide_pairs))
        return apply_pairs(field, (2, 1, 0), self.pairs)


def with_following(guess, edges, after, after_edge):
    fields = [wide(blocks(guess[s]), blocks(edges[s])) for s in range(guess.shape[0])]
    sign = last_sign()
    fields.append(each(lambda part: sign * part, wide(blocks(after[0]), blocks(after_edge[0]))))
    return fields


def residual_kernel(source, guess, bonds, edges, after, after_edge, expo, tables, inner, basis, out):
    slices, rows, _ = guess.shape
    band = Band(bonds, edges, expo, tables, slices)
    field = with_following(guess, edges, after, after_edge)
    pieces = []
    link = field[0]
    for s in range(slices):
        applied = band.propagated(s, blocks(inner[s]), blocks(edges[s]))
        following = each(lax.sub, field[s + 1], applied)
        back = joined(times(band.expo[s], band.pulled(following)))
        pieces.append(source[s] - joined(band.own(link)) + back)
        link = following
    pieces.insert(1, joined(band.own(applied)))
    places = [0, slices] + list(range(1, slices))
    for group in (slice(0, 2), slice(2, None)):
        waves = product(basis, halves(jnp.concatenate(pieces[group], 0)), ROWS_BY_ROWS)
        for i, s in enumerate(places[group]):
            out[:, s * rows : (s + 1) * rows] = waves[:, i * rows : (i + 1) * rows]


def mode_kernel(count, mixed, slices_in, slices_out, rows_in, rims, out):
    tm, band, modes, width = mixed.shape
    size = tm * modes
    freqs = slices_in.shape[1] // modes
    length = rows_in.shape[1]
    per = length // band
    slots = width // per
    chunk = slots * modes + 1

    stacked = jnp.concatenate(
        [
            jnp.concatenate(
                [mixed[:, b, :, s * per : (s + 1) * per].reshape(size, per) for b in range(band)], 1
            )
            for s in range(slots)
        ],
        0,
    )
    waves = product(halves(product(slices_in, halves(stacked))), rows_in)

    place = lax.axis_index("tm") * band + lax.axis_index("band")
    shape = (modes, length)
    column = place * modes + lax.broadcasted_iota(jnp.int32, shape, 0)
    row = lax.broadcasted_iota(jnp.int32, shape, 1)
    sine_c = jnp.sin(((column + 1) // 2).astype(jnp.float32) * (math.pi / count))
    sine_r = jnp.sin(((row + 1) // 2).astype(jnp.float32) * (math.pi / length))
    depth = sine_c * sine_c + sine_r * sine_r
    top = cheb_t(ORDER, 1.0 - depth * (4.0 / half_width))
    gains = []
    for k in range(freqs):
        if k % 2 == 0:
            lift = cheb_slope * (1.0 - math.cos((k + 1) * math.pi / freqs))
            damp = 1.0 / math.cosh(ORDER * math.acosh((cheb_base + lift) / half_width))
            gain = (1.0 - damp * top) / (4.0 * depth + (cheb_base - 4.0 + lift))
        gains.append(gain)
    waves = halves(waves * jnp.concatenate(gains, 0))

    back = product(slices_out, halves(product(waves, rows_in, ROWS_BY_ROWS)))
    edge = product(halves(product(halves(rims[...]), waves, ROWS_BY_ROWS)), slices_in)
    turns = [
        pltpu.roll(edge[:, s * size : (s + 1) * size], RIM * s * modes, 1, stride=modes, stride_axis=0)
        for s in range(slots)
    ]
    group = lax.broadcasted_iota(jnp.int32, (tm, size), 1) // modes
    slot = group - lax.broadcasted_iota(jnp.int32, (tm, size), 0)
    slot = jnp.where(slot < 0, slot + tm, slot)
    for b in range(band):
        rim = jnp.zeros((tm, size), jnp.float32)
        for s in range(slots):
            for q in range(RIM):
                line = turns[s][b * RIM + q : b * RIM + q + 1]
                rim = jnp.where(slot == (RIM * (s + b) + q) % tm, line, rim)
        for p in range(tm):
            at = (p * band + b) * chunk
            for s in range(slots):
                start = s * size + p * modes
                out[at + s * modes : at + (s + 1) * modes] = back[start : start + modes, b * per : (b + 1) * per]
            out[at + slots * modes : at + chunk] = rim[p : p + 1]


def force_kernel(base, guess, bonds, edges, after, after_edge, expo, tables, mixed, basis, order, sol, mom, turned_edge):
    slices, _, cols = guess.shape
    devices = lax.axis_size("tm") * lax.axis_size("band")
    modes = cols // devices
    slots = slices + 1
    chunk = slots * modes + 1
    band = Band(bonds, edges, expo, tables, slices)
    columns = (basis[0], basis[1])

    rim = mixed[pl.ds(slots * modes, devices, stride=chunk), :]
    lanes = rim.shape[1]
    by = modes * (lax.axis_index("tm") + RIM * lax.axis_index("band"))
    rim = pltpu.roll(rim, lax.rem(2 * lanes - by, lanes), 1)
    turned_edge[...] = rim.T
    groups = lanes // modes
    lines = jnp.concatenate([turned_edge[pl.ds(m, groups, stride=modes), :] for m in range(modes)], 1)
    strips = product(halves(lines), order)

    start = with_following(guess, edges, after, after_edge)
    field = []
    for s in range(slots):
        arrived = [mixed[d * chunk + s * modes : d * chunk + (s + 1) * modes] for d in range(devices)]
        timed = product(halves(jnp.concatenate(arrived, 0).T), columns)
        strip = pltpu.roll(strips[s * RIM : s * RIM + HALO], HALO - NEAR, 0)
        change = wide(blocks(timed), blocks(strip))
        field.append(each(lambda old, new: old + relaxation * new, start[s], change))
    for s in range(slices):
        own = band.own(field[s])
        ahead = band.propagated(s, band.inner(s, own), band.rim(field[s]))
        pulled = band.pulled(each(lax.sub, field[s + 1], ahead))
        sol[s] = joined(own)
        fermion = (-2.0 * coupling) * joined(times(times(band.expo[s], own), pulled))
        mom[s] = base[s] - step_size * fermion


def call(kernel, outs, *operands, flops=0, **kwargs):
    vmem = pl.BlockSpec(memory_space=pltpu.VMEM)
    return pl.pallas_call(
        kernel,
        out_shape=outs,
        in_specs=[vmem] * len(operands),
        out_specs=jax.tree.map(lambda _: vmem, outs),
        compiler_params=pltpu.CompilerParams(vmem_limit_bytes=12 << 20),
        cost_estimate=pl.CostEstimate(flops=flops, bytes_accessed=4 << 20, transcendentals=0),
        **kwargs,
    )(*map(onchip, operands))


def onchip(value):
    return pltpu.with_memory_space_constraint(value, pltpu.VMEM)


def pack_kernel(guess, *refs):
    tops, ends, outs = refs[:3], refs[3:6], refs[6:]
    first, rims, rim = outs
    first[...] = guess[...]
    early = lax.broadcasted_iota(jnp.int32, tops[0].shape, 1) < EDGE
    at = 0
    for top, end in zip(tops, ends):
        both = jnp.where(early, top[...], end[...]).astype(jnp.float32)
        rims[at : at + top.shape[0]] = both
        if at == 0:
            rim[...] = both[:1]
        at += top.shape[0]


def pack(phonon, guess, bonds):
    slices, rows, cols = guess.shape
    fields = (guess, phonon, bonds)
    last = rows // HALO - 1
    whole = lambda shape: pl.BlockSpec(shape, lambda i: (0, 0, 0))
    tops = [whole((v.shape[0], HALO, cols)) for v in fields]
    ends = [pl.BlockSpec((v.shape[0], HALO, cols), lambda i: (0, last, 0)) for v in fields]
    outs = [(1, rows, cols), (2 * slices + 2, HALO, cols), (1, HALO, cols)]
    return pl.pallas_call(
        pack_kernel,
        grid=(1,),
        out_shape=[pltpu.VMEM(o, jnp.float32) for o in outs],
        in_specs=[whole((1, rows, cols))] + tops + ends,
        out_specs=[whole(o) for o in outs],
    )(guess, *fields, *fields)


def shards(phonon, momentum, source, guess, bonds):
    slices, rows, cols = guess.shape
    tm, band = lax.axis_size("tm"), lax.axis_size("band")
    total, length, devices = tm * slices, rows * band, tm * band
    modes = cols // devices
    slots = slices + 1

    slot_times = np.concatenate([time_basis(total, slices * np.arange(tm) + s) for s in range(slots)], 1)
    slices_in = np.kron(slot_times, np.eye(modes))
    near = np.concatenate([np.arange(-NEAR, 0), rows + np.arange(NEAR)])
    rim_sites = np.concatenate([(b * rows + near) % length for b in range(band)])
    rims_basis = np.asarray(space_basis(length, rim_sites).T, np.float32)
    rows_in = const_halves(space_basis(length, np.arange(length)).T)
    columns = const_halves(space_basis(cols, np.arange(cols)))

    first, rims, rim = pack(phonon, guess, bonds)
    edges = band_halo(rims, 0)
    after = shifted(first, 1, 0)
    after_edge = band_halo(rim, 1)

    on = lambda *shape: pltpu.VMEM(shape, jnp.float32)
    expo, tables, inner = call(
        local_kernel, (on(slices, rows, cols), on(6, rows, cols), on(slices, rows, cols)),
        phonon, guess, bonds,
    )
    sent = call(
        residual_kernel, jax.ShapeDtypeStruct((cols, slots * rows), jnp.float32),
        source, guess, bonds, edges, after, after_edge, expo, tables, inner, columns,
    )
    mixed = lax.all_to_all(sent.reshape(devices, modes, slots * rows), AXES, 0, 0, tiled=True)
    wave_rows = devices * (slots * modes + 1)
    back = call(
        functools.partial(mode_kernel, cols), on(wave_rows, rows),
        mixed.reshape(tm, band, modes, slots * rows),
        const_halves(slices_in), const_halves(np.ascontiguousarray(slices_in.T)), rows_in, rims_basis,
    )
    mixed = lax.all_to_all(back.reshape(devices, 1, -1), AXES, 0, 0, tiled=True)

    after_ph = shifted(phonon[:1], 1, 0)
    before_ph = shifted(phonon[-1:], -1, 0)
    ring = jnp.concatenate([before_ph, phonon, after_ph], 0)
    boson = stiffness * (2.0 * phonon - ring[:-2] - ring[2:]) + mass_term * phonon
    base = momentum - step_size * boson
    like = jax.ShapeDtypeStruct(guess.shape, jnp.float32)
    return call(
        force_kernel, (like, like),
        base, guess, bonds, edges, after, after_edge, expo, tables,
        mixed.reshape(wave_rows, rows), columns,
        np.ascontiguousarray(columns.reshape(2, devices, modes, cols).swapaxes(1, 2).reshape(2, cols, cols)),
        scratch_shapes=[pltpu.VMEM((cols // band, devices), jnp.float32)],
    )


def solution(mesh):
    spec = P("tm", "band", None)
    return jax.shard_map(
        shards,
        mesh=mesh,
        in_specs=(spec, spec, spec, spec, P(None, "band", None)),
        out_specs=(spec, spec),
        check_vma=False,
    )
```

```python
import functools
import math

import numpy as np

import jax
import jax.numpy as jnp
from jax import lax
from jax.experimental import pallas as pl
from jax.experimental.pallas import tpu as pltpu
from jax.sharding import PartitionSpec as P


ORDER = 24

hop_angle = 0.3
coupling = 0.2
stiffness = 1.0
mass_term = 0.5
relaxation = 0.25
step_size = 0.25
cheb_base = 4.03
cheb_slope = 0.5
half_width = 4.0

EDGE = 4
HALO = 2 * EDGE
SUBLANES = 8
LANES = 128
NEAR = 2
RIM = 2 * NEAR
AXES = ("tm", "band")
ROWS_BY_COLS = (((1,), (0,)), ((), ()))
ROWS_BY_ROWS = (((1,), (1,)), ((), ()))


def shifted(value, dt, db):
    tm, band = lax.axis_size("tm"), lax.axis_size("band")
    pairs = [
        (((t + dt) % tm) * band + (b + db) % band, t * band + b)
        for t in range(tm)
        for b in range(band)
    ]
    return lax.ppermute(value, AXES, pairs)


def band_halo(tile, dt):
    if lax.axis_size("band") == 2:
        return shifted(tile, dt, 1)
    after = shifted(tile[..., :EDGE, :], dt, 1)
    before = shifted(tile[..., EDGE:, :], dt, -1)
    return jnp.concatenate([after, before], -2)


def time_basis(slices, at):
    k = np.arange(slices)[:, None]
    phase = (2 * (k // 2) + 1) * np.asarray(at)[None, :] % (2 * slices)
    angle = phase * (math.pi / slices)
    return math.sqrt(2.0 / slices) * np.where(k % 2 == 0, np.cos(angle), np.sin(angle))


def space_basis(length, at):
    mode = np.arange(length)[:, None]
    freq = (mode + 1) // 2
    angle = (freq * np.asarray(at)[None, :] % length) * (2.0 * math.pi / length)
    wave = np.where((mode % 2 == 0) & (mode > 0), np.sin(angle), np.cos(angle))
    norm = np.where((mode == 0) | (2 * freq == length), 1.0, 2.0)
    return np.sqrt(norm / length) * wave


def cheb_t(order, x):
    if order == 0:
        return jnp.ones_like(x)
    if order == 1:
        return x
    if order % 2 == 0:
        half = cheb_t(order // 2, x)
        return 2.0 * half * half - 1.0
    return 2.0 * cheb_t((order + 1) // 2, x) * cheb_t(order // 2, x) - x


def blocks(value):
    rows, cols = value.shape
    return [value[:, i : i + LANES].reshape(rows // SUBLANES, SUBLANES, LANES) for i in range(0, cols, LANES)]


def joined(parts):
    return jnp.concatenate([part.reshape(-1, LANES) for part in parts], 1)


def each(function, *lists):
    return [function(*items) for items in zip(*lists)]


def taken(part, index):
    numbers = lax.GatherDimensionNumbers(
        offset_dims=(),
        collapsed_slice_dims=(2,),
        start_index_map=(2,),
        operand_batching_dims=(0, 1),
        start_indices_batching_dims=(0, 1),
    )
    return lax.gather(
        part, index[..., None], numbers, (1, 1, 1), mode=lax.GatherScatterMode.PROMISE_IN_BOUNDS
    )


def along_columns(parts, colour):
    place = lax.broadcasted_iota(jnp.int32, parts[0].shape, 2)
    if colour == 0:
        return each(lambda part: taken(part, place ^ 1), parts)
    before, after = parts[-1:] + parts[:-1], parts[1:] + parts[:1]
    if len(parts) == 2:
        outer = (place == 0) | (place == LANES - 1)
        parts = each(lambda mine, other: jnp.where(outer, other, mine), parts, after)
    else:
        parts = each(
            lambda mine, low, high: jnp.where(place == LANES - 1, low, jnp.where(place == 0, high, mine)),
            parts, before, after,
        )
    index = ((((place + LANES - 1) & (LANES - 1)) ^ 1) + 1) & (LANES - 1)
    return each(lambda part: taken(part, index), parts)


def along_rows(parts, colour):
    place = lax.broadcasted_iota(jnp.int32, parts[0].shape, 1)
    even = (place & 1) == 0

    def partner(part):
        up, down = pltpu.roll(part, SUBLANES - 1, 1), pltpu.roll(part, 1, 1)
        if colour == 2:
            return jnp.where(even, up, down)
        inside = jnp.where(even, down, up)
        if part.shape[0] == 1:
            return inside
        low = jnp.concatenate([down[-1:], down[:-1]], 0)
        high = jnp.concatenate([up[1:], up[:1]], 0)
        return jnp.where(place == 0, low, jnp.where(place == SUBLANES - 1, high, inside))

    return each(partner, parts)


def partners(parts, colour):
    return along_columns(parts, colour) if colour < 2 else along_rows(parts, colour)


def pair_table(strengths, colour):
    parts = strengths[colour // 2]
    odd = lax.broadcasted_iota(jnp.int32, parts[0].shape, 2 if colour < 2 else 1) & 1
    holder = odd == colour % 2
    bonds = each(lambda mine, other: jnp.where(holder, mine, other), parts, partners(parts, colour))
    cosh_part = each(lambda bond: 1.0 + (math.cosh(hop_angle) - 1.0) * bond, bonds)
    return cosh_part, each(lambda bond: math.sinh(hop_angle) * bond, bonds)


def apply_pairs(parts, colours, tables):
    for colour in colours:
        mix = lambda mine, other, cosh_part, sinh_part: cosh_part * mine + sinh_part * other
        parts = each(mix, parts, partners(parts, colour), *tables[colour])
    return parts


def last_sign():
    at_end = lax.axis_index("tm") == lax.axis_size("tm") - 1
    return jnp.where(at_end, -1.0, 1.0).astype(jnp.float32)


def halves(value):
    high = value.astype(jnp.bfloat16)
    return high, (value - high.astype(jnp.float32)).astype(jnp.bfloat16)


def const_halves(value):
    high = np.asarray(value, np.float32).astype(jnp.bfloat16)
    low = (value - high.astype(np.float64)).astype(np.float32).astype(jnp.bfloat16)
    return np.stack([high, low])


def product(a, b, dims=ROWS_BY_COLS):
    dot = functools.partial(lax.dot_general, dimension_numbers=dims, preferred_element_type=jnp.float32)
    return dot(a[0], b[0]) + (dot(a[0], b[1]) + dot(a[1], b[0]))


def times(a, b):
    return each(lax.mul, a, b)


def wide(main, halo):
    return each(lambda rows, rim: jnp.concatenate([rows, rim], 0), main, halo)


def local_kernel(phonon, guess, bonds, expo, tables, inner):
    slices = guess.shape[0]
    strengths = [blocks(bonds[d].astype(jnp.float32)) for d in range(2)]
    pairs = [pair_table(strengths, q) for q in range(3)]
    for q in range(3):
        for part in range(2):
            tables[2 * q + part] = joined(pairs[q][part])
    for s in range(slices):
        grown = jnp.exp(-coupling * phonon[s])
        expo[s] = grown
        inner[s] = joined(apply_pairs(blocks(grown * guess[s]), (0, 1, 2), pairs))


class Band:
    def __init__(self, bonds, edges, expo, tables, slices):
        self.tiles = bonds.shape[1] // SUBLANES
        across, down = blocks(edges[2 * slices]), blocks(edges[2 * slices + 1])
        self.pairs = [[blocks(tables[2 * q + part]) for part in range(2)] for q in range(3)]
        self.strip_pairs = [pair_table((across, down), q) for q in range(3)]
        vertical = wide(blocks(bonds[1].astype(jnp.float32)), down)
        self.wide_pairs = {3: pair_table((None, vertical), 3)}
        self.expo = [blocks(expo[s]) for s in range(slices)]
        self.strip_expo = [blocks(jnp.exp(-coupling * edges[slices + s])) for s in range(slices)]

    def own(self, parts):
        return each(lambda part: part[: self.tiles], parts)

    def rim(self, parts):
        return each(lambda part: part[self.tiles :], parts)

    def inner(self, s, field):
        return apply_pairs(times(self.expo[s], field), (0, 1, 2), self.pairs)

    def propagated(self, s, inner, strip):
        strip = apply_pairs(times(self.strip_expo[s], strip), (0, 1, 2), self.strip_pairs)
        return apply_pairs(wide(inner, strip), (3,), self.wide_pairs)

    def pulled(self, field):
        field = self.own(apply_pairs(field, (3,), self.wide_pairs))
        return apply_pairs(field, (2, 1, 0), self.pairs)


def with_following(guess, edges, after, after_edge):
    fields = [wide(blocks(guess[s]), blocks(edges[s])) for s in range(guess.shape[0])]
    sign = last_sign()
    fields.append(each(lambda part: sign * part, wide(blocks(after[0]), blocks(after_edge[0]))))
    return fields


def residual_kernel(source, guess, bonds, edges, after, after_edge, expo, tables, inner, basis, out):
    slices, rows, _ = guess.shape
    band = Band(bonds, edges, expo, tables, slices)
    field = with_following(guess, edges, after, after_edge)
    pieces = []
    link = field[0]
    for s in range(slices):
        applied = band.propagated(s, blocks(inner[s]), blocks(edges[s]))
        following = each(lax.sub, field[s + 1], applied)
        back = joined(times(band.expo[s], band.pulled(following)))
        pieces.append(source[s] - joined(band.own(link)) + back)
        link = following
    pieces.insert(1, joined(band.own(applied)))
    places = [0, slices] + list(range(1, slices))
    for group in (slice(0, 2), slice(2, None)):
        waves = product(basis, halves(jnp.concatenate(pieces[group], 0)), ROWS_BY_ROWS)
        for i, s in enumerate(places[group]):
            out[:, s * rows : (s + 1) * rows] = waves[:, i * rows : (i + 1) * rows]


def mode_kernel(count, mixed, slices_in, slices_out, rows_in, rims, out):
    tm, band, modes, width = mixed.shape
    size = tm * modes
    freqs = slices_in.shape[1] // modes
    length = rows_in.shape[1]
    per = length // band
    slots = width // per
    chunk = slots * modes + 1

    stacked = jnp.concatenate(
        [
            jnp.concatenate(
                [mixed[:, b, :, s * per : (s + 1) * per].reshape(size, per) for b in range(band)], 1
            )
            for s in range(slots)
        ],
        0,
    )
    waves = product(halves(product(slices_in, halves(stacked))), rows_in)

    place = lax.axis_index("tm") * band + lax.axis_index("band")
    shape = (modes, length)
    column = place * modes + lax.broadcasted_iota(jnp.int32, shape, 0)
    row = lax.broadcasted_iota(jnp.int32, shape, 1)
    sine_c = jnp.sin(((column + 1) // 2).astype(jnp.float32) * (math.pi / count))
    sine_r = jnp.sin(((row + 1) // 2).astype(jnp.float32) * (math.pi / length))
    depth = sine_c * sine_c + sine_r * sine_r
    top = cheb_t(ORDER, 1.0 - depth * (4.0 / half_width))
    gains = []
    for k in range(freqs):
        if k % 2 == 0:
            lift = cheb_slope * (1.0 - math.cos((k + 1) * math.pi / freqs))
            damp = 1.0 / math.cosh(ORDER * math.acosh((cheb_base + lift) / half_width))
            gain = (1.0 - damp * top) / (4.0 * depth + (cheb_base - 4.0 + lift))
        gains.append(gain)
    waves = halves(waves * jnp.concatenate(gains, 0))

    back = product(slices_out, halves(product(waves, rows_in, ROWS_BY_ROWS)))
    edge = product(halves(product(halves(rims[...]), waves, ROWS_BY_ROWS)), slices_in)
    turns = [
        pltpu.roll(edge[:, s * size : (s + 1) * size], RIM * s * modes, 1, stride=modes, stride_axis=0)
        for s in range(slots)
    ]
    group = lax.broadcasted_iota(jnp.int32, (tm, size), 1) // modes
    slot = group - lax.broadcasted_iota(jnp.int32, (tm, size), 0)
    slot = jnp.where(slot < 0, slot + tm, slot)
    for b in range(band):
        rim = jnp.zeros((tm, size), jnp.float32)
        for s in range(slots):
            for q in range(RIM):
                line = turns[s][b * RIM + q : b * RIM + q + 1]
                rim = jnp.where(slot == (RIM * (s + b) + q) % tm, line, rim)
        for p in range(tm):
            at = (p * band + b) * chunk
            for s in range(slots):
                start = s * size + p * modes
                out[at + s * modes : at + (s + 1) * modes] = back[start : start + modes, b * per : (b + 1) * per]
            out[at + slots * modes : at + chunk] = rim[p : p + 1]


def force_kernel(base, guess, bonds, edges, after, after_edge, expo, tables, mixed, basis, order, sol, mom, turned_edge):
    slices, _, cols = guess.shape
    devices = lax.axis_size("tm") * lax.axis_size("band")
    modes = cols // devices
    slots = slices + 1
    chunk = slots * modes + 1
    band = Band(bonds, edges, expo, tables, slices)
    columns = (basis[0], basis[1])

    rim = mixed[pl.ds(slots * modes, devices, stride=chunk), :]
    lanes = rim.shape[1]
    by = modes * (lax.axis_index("tm") + RIM * lax.axis_index("band"))
    rim = pltpu.roll(rim, lax.rem(2 * lanes - by, lanes), 1)
    turned_edge[...] = rim.T
    groups = lanes // modes
    lines = jnp.concatenate([turned_edge[pl.ds(m, groups, stride=modes), :] for m in range(modes)], 1)
    strips = product(halves(lines), order)

    start = with_following(guess, edges, after, after_edge)
    field = []
    for s in range(slots):
        arrived = [mixed[d * chunk + s * modes : d * chunk + (s + 1) * modes] for d in range(devices)]
        timed = product(halves(jnp.concatenate(arrived, 0).T), columns)
        strip = pltpu.roll(strips[s * RIM : s * RIM + HALO], HALO - NEAR, 0)
        change = wide(blocks(timed), blocks(strip))
        field.append(each(lambda old, new: old + relaxation * new, start[s], change))
    for s in range(slices):
        own = band.own(field[s])
        ahead = band.propagated(s, band.inner(s, own), band.rim(field[s]))
        pulled = band.pulled(each(lax.sub, field[s + 1], ahead))
        sol[s] = joined(own)
        fermion = (-2.0 * coupling) * joined(times(times(band.expo[s], own), pulled))
        mom[s] = base[s] - step_size * fermion


def call(kernel, outs, *operands, flops=0, **kwargs):
    vmem = pl.BlockSpec(memory_space=pltpu.VMEM)
    return pl.pallas_call(
        kernel,
        out_shape=outs,
        in_specs=[vmem] * len(operands),
        out_specs=jax.tree.map(lambda _: vmem, outs),
        compiler_params=pltpu.CompilerParams(vmem_limit_bytes=12 << 20),
        cost_estimate=pl.CostEstimate(flops=flops, bytes_accessed=4 << 20, transcendentals=0),
        **kwargs,
    )(*map(onchip, operands))


def onchip(value):
    return pltpu.with_memory_space_constraint(value, pltpu.VMEM)


def pack_kernel(guess, *refs):
    last_ph, tops, ends, outs = refs[0], refs[1:4], refs[4:7], refs[7:]
    first, last, rims, rim = outs
    first[...] = guess[...]
    last[...] = last_ph[...]
    early = lax.broadcasted_iota(jnp.int32, tops[0].shape, 1) < EDGE
    at = 0
    for top, end in zip(tops, ends):
        both = jnp.where(early, top[...], end[...]).astype(jnp.float32)
        rims[at : at + top.shape[0]] = both
        if at == 0:
            rim[...] = both[:1]
        at += top.shape[0]


def pack(phonon, guess, bonds):
    slices, rows, cols = guess.shape
    fields = (guess, phonon, bonds)
    last = rows // HALO - 1
    whole = lambda shape: pl.BlockSpec(shape, lambda i: (0, 0, 0))
    tops = [whole((v.shape[0], HALO, cols)) for v in fields]
    ends = [pl.BlockSpec((v.shape[0], HALO, cols), lambda i: (0, last, 0)) for v in fields]
    outs = [(1, rows, cols), (1, rows, cols), (2 * slices + 2, HALO, cols), (1, HALO, cols)]
    final = pl.BlockSpec((1, rows, cols), lambda i: (slices - 1, 0, 0))
    return pl.pallas_call(
        pack_kernel,
        grid=(1,),
        out_shape=[pltpu.VMEM(o, jnp.float32) for o in outs],
        in_specs=[whole((1, rows, cols)), final] + tops + ends,
        out_specs=[whole(o) for o in outs],
    )(guess, phonon, *fields, *fields)


def shards(phonon, momentum, source, guess, bonds):
    slices, rows, cols = guess.shape
    tm, band = lax.axis_size("tm"), lax.axis_size("band")
    total, length, devices = tm * slices, rows * band, tm * band
    modes = cols // devices
    slots = slices + 1

    slot_times = np.concatenate([time_basis(total, slices * np.arange(tm) + s) for s in range(slots)], 1)
    slices_in = np.kron(slot_times, np.eye(modes))
    near = np.concatenate([np.arange(-NEAR, 0), rows + np.arange(NEAR)])
    rim_sites = np.concatenate([(b * rows + near) % length for b in range(band)])
    rims_basis = np.asarray(space_basis(length, rim_sites).T, np.float32)
    rows_in = const_halves(space_basis(length, np.arange(length)).T)
    columns = const_halves(space_basis(cols, np.arange(cols)))

    first, last, rims, rim = pack(phonon, guess, bonds)
    edges = band_halo(rims, 0)
    after = shifted(first, 1, 0)
    after_edge = band_halo(rim, 1)

    on = lambda *shape: pltpu.VMEM(shape, jnp.float32)
    expo, tables, inner = call(
        local_kernel, (on(slices, rows, cols), on(6, rows, cols), on(slices, rows, cols)),
        phonon, guess, bonds,
    )
    sent = call(
        residual_kernel, jax.ShapeDtypeStruct((cols, slots * rows), jnp.float32),
        source, guess, bonds, edges, after, after_edge, expo, tables, inner, columns,
    )
    mixed = lax.all_to_all(sent.reshape(devices, modes, slots * rows), AXES, 0, 0, tiled=True)
    wave_rows = devices * (slots * modes + 1)
    back = call(
        functools.partial(mode_kernel, cols), on(wave_rows, rows),
        mixed.reshape(tm, band, modes, slots * rows),
        const_halves(slices_in), const_halves(np.ascontiguousarray(slices_in.T)), rows_in, rims_basis,
    )
    mixed = lax.all_to_all(back.reshape(devices, 1, -1), AXES, 0, 0, tiled=True)

    after_ph = shifted(phonon[:1], 1, 0)
    before_ph = shifted(last, -1, 0)
    ring = jnp.concatenate([before_ph, phonon, after_ph], 0)
    boson = stiffness * (2.0 * phonon - ring[:-2] - ring[2:]) + mass_term * phonon
    base = momentum - step_size * boson
    like = jax.ShapeDtypeStruct(guess.shape, jnp.float32)
    return call(
        force_kernel, (like, like),
        base, guess, bonds, edges, after, after_edge, expo, tables,
        mixed.reshape(wave_rows, rows), columns,
        np.ascontiguousarray(columns.reshape(2, devices, modes, cols).swapaxes(1, 2).reshape(2, cols, cols)),
        scratch_shapes=[pltpu.VMEM((cols // band, devices), jnp.float32)],
    )


def solution(mesh):
    spec = P("tm", "band", None)
    return jax.shard_map(
        shards,
        mesh=mesh,
        in_specs=(spec, spec, spec, spec, P(None, "band", None)),
        out_specs=(spec, spec),
        check_vma=False,
    )
```

```python
import functools
import math

import numpy as np

import jax
import jax.numpy as jnp
from jax import lax
from jax.experimental import pallas as pl
from jax.experimental.pallas import tpu as pltpu
from jax.sharding import PartitionSpec as P


ORDER = 24

hop_angle = 0.3
coupling = 0.2
stiffness = 1.0
mass_term = 0.5
relaxation = 0.25
step_size = 0.25
cheb_base = 4.03
cheb_slope = 0.5
half_width = 4.0

EDGE = 4
HALO = 2 * EDGE
SUBLANES = 8
LANES = 128
NEAR = 2
RIM = 2 * NEAR
AXES = ("tm", "band")
ROWS_BY_COLS = (((1,), (0,)), ((), ()))
ROWS_BY_ROWS = (((1,), (1,)), ((), ()))


def shifted(value, dt, db):
    tm, band = lax.axis_size("tm"), lax.axis_size("band")
    pairs = [
        (((t + dt) % tm) * band + (b + db) % band, t * band + b)
        for t in range(tm)
        for b in range(band)
    ]
    return lax.ppermute(value, AXES, pairs)


def band_halo(tile, dt):
    if lax.axis_size("band") == 2:
        return shifted(tile, dt, 1)
    after = shifted(tile[..., :EDGE, :], dt, 1)
    before = shifted(tile[..., EDGE:, :], dt, -1)
    return jnp.concatenate([after, before], -2)


def time_basis(slices, at):
    k = np.arange(slices)[:, None]
    phase = (2 * (k // 2) + 1) * np.asarray(at)[None, :] % (2 * slices)
    angle = phase * (math.pi / slices)
    return math.sqrt(2.0 / slices) * np.where(k % 2 == 0, np.cos(angle), np.sin(angle))


def space_basis(length, at):
    mode = np.arange(length)[:, None]
    freq = (mode + 1) // 2
    angle = (freq * np.asarray(at)[None, :] % length) * (2.0 * math.pi / length)
    wave = np.where((mode % 2 == 0) & (mode > 0), np.sin(angle), np.cos(angle))
    norm = np.where((mode == 0) | (2 * freq == length), 1.0, 2.0)
    return np.sqrt(norm / length) * wave


def cheb_t(order, x):
    if order == 0:
        return jnp.ones_like(x)
    if order == 1:
        return x
    if order % 2 == 0:
        half = cheb_t(order // 2, x)
        return 2.0 * half * half - 1.0
    return 2.0 * cheb_t((order + 1) // 2, x) * cheb_t(order // 2, x) - x


def blocks(value):
    rows, cols = value.shape
    return [value[:, i : i + LANES].reshape(rows // SUBLANES, SUBLANES, LANES) for i in range(0, cols, LANES)]


def joined(parts):
    return jnp.concatenate([part.reshape(-1, LANES) for part in parts], 1)


def each(function, *lists):
    return [function(*items) for items in zip(*lists)]


def taken(part, index):
    numbers = lax.GatherDimensionNumbers(
        offset_dims=(),
        collapsed_slice_dims=(2,),
        start_index_map=(2,),
        operand_batching_dims=(0, 1),
        start_indices_batching_dims=(0, 1),
    )
    return lax.gather(
        part, index[..., None], numbers, (1, 1, 1), mode=lax.GatherScatterMode.PROMISE_IN_BOUNDS
    )


def along_columns(parts, colour):
    place = lax.broadcasted_iota(jnp.int32, parts[0].shape, 2)
    if colour == 0:
        return each(lambda part: taken(part, place ^ 1), parts)
    before, after = parts[-1:] + parts[:-1], parts[1:] + parts[:1]
    if len(parts) == 2:
        outer = (place == 0) | (place == LANES - 1)
        parts = each(lambda mine, other: jnp.where(outer, other, mine), parts, after)
    else:
        parts = each(
            lambda mine, low, high: jnp.where(place == LANES - 1, low, jnp.where(place == 0, high, mine)),
            parts, before, after,
        )
    index = ((((place + LANES - 1) & (LANES - 1)) ^ 1) + 1) & (LANES - 1)
    return each(lambda part: taken(part, index), parts)


def along_rows(parts, colour):
    place = lax.broadcasted_iota(jnp.int32, parts[0].shape, 1)
    even = (place & 1) == 0

    def partner(part):
        up, down = pltpu.roll(part, SUBLANES - 1, 1), pltpu.roll(part, 1, 1)
        if colour == 2:
            return jnp.where(even, up, down)
        inside = jnp.where(even, down, up)
        if part.shape[0] == 1:
            return inside
        low = jnp.concatenate([down[-1:], down[:-1]], 0)
        high = jnp.concatenate([up[1:], up[:1]], 0)
        return jnp.where(place == 0, low, jnp.where(place == SUBLANES - 1, high, inside))

    return each(partner, parts)


def partners(parts, colour):
    return along_columns(parts, colour) if colour < 2 else along_rows(parts, colour)


def pair_table(strengths, colour):
    parts = strengths[colour // 2]
    odd = lax.broadcasted_iota(jnp.int32, parts[0].shape, 2 if colour < 2 else 1) & 1
    holder = odd == colour % 2
    bonds = each(lambda mine, other: jnp.where(holder, mine, other), parts, partners(parts, colour))
    cosh_part = each(lambda bond: 1.0 + (math.cosh(hop_angle) - 1.0) * bond, bonds)
    return cosh_part, each(lambda bond: math.sinh(hop_angle) * bond, bonds)


def apply_pairs(parts, colours, tables):
    for colour in colours:
        mix = lambda mine, other, cosh_part, sinh_part: cosh_part * mine + sinh_part * other
        parts = each(mix, parts, partners(parts, colour), *tables[colour])
    return parts


def last_sign():
    at_end = lax.axis_index("tm") == lax.axis_size("tm") - 1
    return jnp.where(at_end, -1.0, 1.0).astype(jnp.float32)


def halves(value):
    high = value.astype(jnp.bfloat16)
    return high, (value - high.astype(jnp.float32)).astype(jnp.bfloat16)


def const_halves(value):
    high = np.asarray(value, np.float32).astype(jnp.bfloat16)
    low = (value - high.astype(np.float64)).astype(np.float32).astype(jnp.bfloat16)
    return np.stack([high, low])


def product(a, b, dims=ROWS_BY_COLS):
    dot = functools.partial(lax.dot_general, dimension_numbers=dims, preferred_element_type=jnp.float32)
    high, low = a[0], a[1]
    rows = high.shape[0]
    cuts = [0, rows // 2 // (2 * SUBLANES) * (2 * SUBLANES), rows]
    parts = []
    for start, stop in zip(cuts, cuts[1:]):
        if start < stop:
            both = dot(jnp.concatenate([high[start:stop], low[start:stop]], 0), b[0])
            small = both[stop - start :] + dot(high[start:stop], b[1])
            parts.append(both[: stop - start] + small)
    return jnp.concatenate(parts, 0)


def times(a, b):
    return each(lax.mul, a, b)


def wide(main, halo):
    return each(lambda rows, rim: jnp.concatenate([rows, rim], 0), main, halo)


def local_kernel(phonon, guess, bonds, expo, tables, inner):
    slices = guess.shape[0]
    strengths = [blocks(bonds[d].astype(jnp.float32)) for d in range(2)]
    pairs = [pair_table(strengths, q) for q in range(3)]
    for q in range(3):
        for part in range(2):
            tables[2 * q + part] = joined(pairs[q][part])
    for s in range(slices):
        grown = jnp.exp(-coupling * phonon[s])
        expo[s] = grown
        inner[s] = joined(apply_pairs(blocks(grown * guess[s]), (0, 1, 2), pairs))


class Band:
    def __init__(self, bonds, edges, expo, tables, slices):
        self.tiles = bonds.shape[1] // SUBLANES
        across, down = blocks(edges[2 * slices]), blocks(edges[2 * slices + 1])
        self.pairs = [[blocks(tables[2 * q + part]) for part in range(2)] for q in range(3)]
        self.strip_pairs = [pair_table((across, down), q) for q in range(3)]
        vertical = wide(blocks(bonds[1].astype(jnp.float32)), down)
        self.wide_pairs = {3: pair_table((None, vertical), 3)}
        self.expo = [blocks(expo[s]) for s in range(slices)]
        self.strip_expo = [blocks(jnp.exp(-coupling * edges[slices + s])) for s in range(slices)]

    def own(self, parts):
        return each(lambda part: part[: self.tiles], parts)

    def rim(self, parts):
        return each(lambda part: part[self.tiles :], parts)

    def inner(self, s, field):
        return apply_pairs(times(self.expo[s], field), (0, 1, 2), self.pairs)

    def propagated(self, s, inner, strip):
        strip = apply_pairs(times(self.strip_expo[s], strip), (0, 1, 2), self.strip_pairs)
        return apply_pairs(wide(inner, strip), (3,), self.wide_pairs)

    def pulled(self, field):
        field = self.own(apply_pairs(field, (3,), self.wide_pairs))
        return apply_pairs(field, (2, 1, 0), self.pairs)


def with_following(guess, edges, after, after_edge):
    fields = [wide(blocks(guess[s]), blocks(edges[s])) for s in range(guess.shape[0])]
    sign = last_sign()
    fields.append(each(lambda part: sign * part, wide(blocks(after[0]), blocks(after_edge[0]))))
    return fields


def residual_kernel(source, guess, bonds, edges, after, after_edge, expo, tables, inner, basis, out):
    slices, rows, _ = guess.shape
    band = Band(bonds, edges, expo, tables, slices)
    field = with_following(guess, edges, after, after_edge)
    pieces = []
    link = field[0]
    for s in range(slices):
        applied = band.propagated(s, blocks(inner[s]), blocks(edges[s]))
        following = each(lax.sub, field[s + 1], applied)
        back = joined(times(band.expo[s], band.pulled(following)))
        pieces.append(source[s] - joined(band.own(link)) + back)
        link = following
    pieces.insert(1, joined(band.own(applied)))
    places = [0, slices] + list(range(1, slices))
    for group in (slice(0, 2), slice(2, None)):
        waves = product(basis, halves(jnp.concatenate(pieces[group], 0)), ROWS_BY_ROWS)
        for i, s in enumerate(places[group]):
            out[:, s * rows : (s + 1) * rows] = waves[:, i * rows : (i + 1) * rows]


def mode_kernel(count, mixed, slices_in, slices_out, rows_in, rows_out, out):
    tm, band, modes, width = mixed.shape
    size = tm * modes
    freqs = slices_in.shape[1] // modes
    length = rows_in.shape[1]
    per = length // band
    slots = width // per
    chunk = slots * modes + 1

    stacked = jnp.concatenate(
        [
            jnp.concatenate(
                [mixed[:, b, :, s * per : (s + 1) * per].reshape(size, per) for b in range(band)], 1
            )
            for s in range(slots)
        ],
        0,
    )
    waves = product(halves(product(slices_in, halves(stacked))), rows_in)

    place = lax.axis_index("tm") * band + lax.axis_index("band")
    shape = (modes, length)
    column = place * modes + lax.broadcasted_iota(jnp.int32, shape, 0)
    row = lax.broadcasted_iota(jnp.int32, shape, 1)
    sine_c = jnp.sin(((column + 1) // 2).astype(jnp.float32) * (math.pi / count))
    sine_r = jnp.sin(((row + 1) // 2).astype(jnp.float32) * (math.pi / length))
    depth = sine_c * sine_c + sine_r * sine_r
    top = cheb_t(ORDER, 1.0 - depth * (4.0 / half_width))
    gains = []
    for k in range(freqs):
        if k % 2 == 0:
            lift = cheb_slope * (1.0 - math.cos((k + 1) * math.pi / freqs))
            damp = 1.0 / math.cosh(ORDER * math.acosh((cheb_base + lift) / half_width))
            gain = (1.0 - damp * top) / (4.0 * depth + (cheb_base - 4.0 + lift))
        gains.append(gain)
    waves = halves(waves * jnp.concatenate(gains, 0))

    lines = halves(product(rows_out, waves, ROWS_BY_ROWS))
    back = product(slices_out, [part[:length] for part in lines], ROWS_BY_ROWS)
    edge = product([part[length:] for part in lines], slices_out, ROWS_BY_ROWS)[: RIM * band]
    turns = [
        pltpu.roll(edge[:, s * size : (s + 1) * size], RIM * s * modes, 1, stride=modes, stride_axis=0)
        for s in range(slots)
    ]
    group = lax.broadcasted_iota(jnp.int32, (tm, size), 1) // modes
    slot = group - lax.broadcasted_iota(jnp.int32, (tm, size), 0)
    slot = jnp.where(slot < 0, slot + tm, slot)
    for b in range(band):
        rim = jnp.zeros((tm, size), jnp.float32)
        for s in range(slots):
            for q in range(RIM):
                line = turns[s][b * RIM + q : b * RIM + q + 1]
                rim = jnp.where(slot == (RIM * (s + b) + q) % tm, line, rim)
        for p in range(tm):
            at = (p * band + b) * chunk
            for s in range(slots):
                start = s * size + p * modes
                out[at + s * modes : at + (s + 1) * modes] = back[start : start + modes, b * per : (b + 1) * per]
            out[at + slots * modes : at + chunk] = rim[p : p + 1]


def force_kernel(base, guess, bonds, edges, after, after_edge, expo, tables, mixed, order, sol, mom, turned_edge):
    slices, rows, cols = guess.shape
    devices = lax.axis_size("tm") * lax.axis_size("band")
    modes = cols // devices
    slots = slices + 1
    chunk = slots * modes + 1
    band = Band(bonds, edges, expo, tables, slices)

    rim = mixed[pl.ds(slots * modes, devices, stride=chunk), :]
    lanes = rim.shape[1]
    by = modes * (lax.axis_index("tm") + RIM * lax.axis_index("band"))
    rim = pltpu.roll(rim, lax.rem(2 * lanes - by, lanes), 1)
    turned_edge[...] = rim.T
    groups = lanes // modes
    lines = jnp.concatenate([turned_edge[pl.ds(m, groups, stride=modes), :] for m in range(modes)], 1)
    arrived = [
        jnp.concatenate([mixed[pl.ds(s * modes + m, devices, stride=chunk), :] for m in range(modes)], 0).T
        for s in range(slots)
    ]
    timed = product(halves(jnp.concatenate(arrived + [lines], 0)), order)
    strips = timed[slots * rows :]

    start = with_following(guess, edges, after, after_edge)
    field = []
    for s in range(slots):
        strip = pltpu.roll(strips[s * RIM : s * RIM + HALO], HALO - NEAR, 0)
        change = wide(blocks(timed[s * rows : (s + 1) * rows]), blocks(strip))
        field.append(each(lambda old, new: old + relaxation * new, start[s], change))
    for s in range(slices):
        own = band.own(field[s])
        ahead = band.propagated(s, band.inner(s, own), band.rim(field[s]))
        pulled = band.pulled(each(lax.sub, field[s + 1], ahead))
        sol[s] = joined(own)
        fermion = (-2.0 * coupling) * joined(times(times(band.expo[s], own), pulled))
        mom[s] = base[s] - step_size * fermion


def call(kernel, outs, *operands, flops=0, **kwargs):
    vmem = pl.BlockSpec(memory_space=pltpu.VMEM)
    return pl.pallas_call(
        kernel,
        out_shape=outs,
        in_specs=[vmem] * len(operands),
        out_specs=jax.tree.map(lambda _: vmem, outs),
        compiler_params=pltpu.CompilerParams(vmem_limit_bytes=12 << 20),
        cost_estimate=pl.CostEstimate(flops=flops, bytes_accessed=4 << 20, transcendentals=0),
        **kwargs,
    )(*map(onchip, operands))


def onchip(value):
    return pltpu.with_memory_space_constraint(value, pltpu.VMEM)


def pack_kernel(guess, *refs):
    last_ph, tops, ends, outs = refs[0], refs[1:4], refs[4:7], refs[7:]
    first, last, rims, rim = outs
    first[...] = guess[...]
    last[...] = last_ph[...]
    early = lax.broadcasted_iota(jnp.int32, tops[0].shape, 1) < EDGE
    at = 0
    for top, end in zip(tops, ends):
        both = jnp.where(early, top[...], end[...]).astype(jnp.float32)
        rims[at : at + top.shape[0]] = both
        if at == 0:
            rim[...] = both[:1]
        at += top.shape[0]


def pack(phonon, guess, bonds):
    slices, rows, cols = guess.shape
    fields = (guess, phonon, bonds)
    last = rows // HALO - 1
    whole = lambda shape: pl.BlockSpec(shape, lambda i: (0, 0, 0))
    tops = [whole((v.shape[0], HALO, cols)) for v in fields]
    ends = [pl.BlockSpec((v.shape[0], HALO, cols), lambda i: (0, last, 0)) for v in fields]
    outs = [(1, rows, cols), (1, rows, cols), (2 * slices + 2, HALO, cols), (1, HALO, cols)]
    final = pl.BlockSpec((1, rows, cols), lambda i: (slices - 1, 0, 0))
    return pl.pallas_call(
        pack_kernel,
        grid=(1,),
        out_shape=[pltpu.VMEM(o, jnp.float32) for o in outs],
        in_specs=[whole((1, rows, cols)), final] + tops + ends,
        out_specs=[whole(o) for o in outs],
    )(guess, phonon, *fields, *fields)


def shards(phonon, momentum, source, guess, bonds):
    slices, rows, cols = guess.shape
    tm, band = lax.axis_size("tm"), lax.axis_size("band")
    total, length, devices = tm * slices, rows * band, tm * band
    modes = cols // devices
    slots = slices + 1

    slot_times = np.concatenate([time_basis(total, slices * np.arange(tm) + s) for s in range(slots)], 1)
    slices_in = np.kron(slot_times, np.eye(modes))
    near = np.concatenate([np.arange(-NEAR, 0), rows + np.arange(NEAR)])
    rim_sites = np.concatenate([(b * rows + near) % length for b in range(band)])
    spare = np.zeros(-len(rim_sites) % (2 * SUBLANES), rim_sites.dtype)
    rows_out = const_halves(space_basis(length, np.concatenate([np.arange(length), rim_sites, spare])).T)
    rows_in = const_halves(space_basis(length, np.arange(length)).T)
    columns = const_halves(space_basis(cols, np.arange(cols)))

    first, last, rims, rim = pack(phonon, guess, bonds)
    edges = band_halo(rims, 0)
    after = shifted(first, 1, 0)
    after_edge = band_halo(rim, 1)

    on = lambda *shape: pltpu.VMEM(shape, jnp.float32)
    expo, tables, inner = call(
        local_kernel, (on(slices, rows, cols), on(6, rows, cols), on(slices, rows, cols)),
        phonon, guess, bonds,
    )
    sent = call(
        residual_kernel, jax.ShapeDtypeStruct((cols, slots * rows), jnp.float32),
        source, guess, bonds, edges, after, after_edge, expo, tables, inner, columns,
    )
    mixed = lax.all_to_all(sent.reshape(devices, modes, slots * rows), AXES, 0, 0, tiled=True)
    wave_rows = devices * (slots * modes + 1)
    back = call(
        functools.partial(mode_kernel, cols), on(wave_rows, rows),
        mixed.reshape(tm, band, modes, slots * rows),
        const_halves(slices_in), const_halves(np.ascontiguousarray(slices_in.T)), rows_in, rows_out,
    )
    mixed = lax.all_to_all(back.reshape(devices, 1, -1), AXES, 0, 0, tiled=True)

    after_ph = shifted(phonon[:1], 1, 0)
    before_ph = shifted(last, -1, 0)
    ring = jnp.concatenate([before_ph, phonon, after_ph], 0)
    boson = stiffness * (2.0 * phonon - ring[:-2] - ring[2:]) + mass_term * phonon
    base = momentum - step_size * boson
    like = jax.ShapeDtypeStruct(guess.shape, jnp.float32)
    return call(
        force_kernel, (like, like),
        base, guess, bonds, edges, after, after_edge, expo, tables,
        mixed.reshape(wave_rows, rows),
        np.ascontiguousarray(columns.reshape(2, devices, modes, cols).swapaxes(1, 2).reshape(2, cols, cols)),
        scratch_shapes=[pltpu.VMEM((cols // band, devices), jnp.float32)],
    )


def solution(mesh):
    spec = P("tm", "band", None)
    return jax.shard_map(
        shards,
        mesh=mesh,
        in_specs=(spec, spec, spec, spec, P(None, "band", None)),
        out_specs=(spec, spec),
        check_vma=False,
    )
```

```python
import functools
import math

import numpy as np

import jax
import jax.numpy as jnp
from jax import lax
from jax.experimental import pallas as pl
from jax.experimental.pallas import tpu as pltpu
from jax.sharding import PartitionSpec as P


ORDER = 24

hop_angle = 0.3
coupling = 0.2
stiffness = 1.0
mass_term = 0.5
relaxation = 0.25
step_size = 0.25
cheb_base = 4.03
cheb_slope = 0.5
half_width = 4.0

EDGE = 4
HALO = 2 * EDGE
SUBLANES = 8
LANES = 128
NEAR = 2
RIM = 2 * NEAR
AXES = ("tm", "band")
EXCHANGE = ("band", "tm")
ROWS_BY_COLS = (((1,), (0,)), ((), ()))
ROWS_BY_ROWS = (((1,), (1,)), ((), ()))


def shifted(value, dt, db):
    tm, band = lax.axis_size("tm"), lax.axis_size("band")
    pairs = [
        (((t + dt) % tm) * band + (b + db) % band, t * band + b)
        for t in range(tm)
        for b in range(band)
    ]
    return lax.ppermute(value, AXES, pairs)


def band_halo(tile, dt):
    if lax.axis_size("band") == 2:
        return shifted(tile, dt, 1)
    after = shifted(tile[..., :EDGE, :], dt, 1)
    before = shifted(tile[..., EDGE:, :], dt, -1)
    return jnp.concatenate([after, before], -2)


def time_basis(slices, at):
    k = np.arange(slices)[:, None]
    phase = (2 * (k // 2) + 1) * np.asarray(at)[None, :] % (2 * slices)
    angle = phase * (math.pi / slices)
    return math.sqrt(2.0 / slices) * np.where(k % 2 == 0, np.cos(angle), np.sin(angle))


def space_basis(length, at):
    mode = np.arange(length)[:, None]
    freq = (mode + 1) // 2
    angle = (freq * np.asarray(at)[None, :] % length) * (2.0 * math.pi / length)
    wave = np.where((mode % 2 == 0) & (mode > 0), np.sin(angle), np.cos(angle))
    norm = np.where((mode == 0) | (2 * freq == length), 1.0, 2.0)
    return np.sqrt(norm / length) * wave


def cheb_t(order, x):
    if order == 0:
        return jnp.ones_like(x)
    if order == 1:
        return x
    if order % 2 == 0:
        half = cheb_t(order // 2, x)
        return 2.0 * half * half - 1.0
    return 2.0 * cheb_t((order + 1) // 2, x) * cheb_t(order // 2, x) - x


def blocks(value):
    rows, cols = value.shape
    return [value[:, i : i + LANES].reshape(rows // SUBLANES, SUBLANES, LANES) for i in range(0, cols, LANES)]


def joined(parts):
    return jnp.concatenate([part.reshape(-1, LANES) for part in parts], 1)


def each(function, *lists):
    return [function(*items) for items in zip(*lists)]


def taken(part, index):
    numbers = lax.GatherDimensionNumbers(
        offset_dims=(),
        collapsed_slice_dims=(2,),
        start_index_map=(2,),
        operand_batching_dims=(0, 1),
        start_indices_batching_dims=(0, 1),
    )
    return lax.gather(
        part, index[..., None], numbers, (1, 1, 1), mode=lax.GatherScatterMode.PROMISE_IN_BOUNDS
    )


def along_columns(parts, colour):
    place = lax.broadcasted_iota(jnp.int32, parts[0].shape, 2)
    if colour == 0:
        return each(lambda part: taken(part, place ^ 1), parts)
    before, after = parts[-1:] + parts[:-1], parts[1:] + parts[:1]
    if len(parts) == 2:
        outer = (place == 0) | (place == LANES - 1)
        parts = each(lambda mine, other: jnp.where(outer, other, mine), parts, after)
    else:
        parts = each(
            lambda mine, low, high: jnp.where(place == LANES - 1, low, jnp.where(place == 0, high, mine)),
            parts, before, after,
        )
    index = ((((place + LANES - 1) & (LANES - 1)) ^ 1) + 1) & (LANES - 1)
    return each(lambda part: taken(part, index), parts)


def along_rows(parts, colour):
    place = lax.broadcasted_iota(jnp.int32, parts[0].shape, 1)
    even = (place & 1) == 0

    def partner(part):
        up, down = pltpu.roll(part, SUBLANES - 1, 1), pltpu.roll(part, 1, 1)
        if colour == 2:
            return jnp.where(even, up, down)
        inside = jnp.where(even, down, up)
        if part.shape[0] == 1:
            return inside
        low = jnp.concatenate([down[-1:], down[:-1]], 0)
        high = jnp.concatenate([up[1:], up[:1]], 0)
        return jnp.where(place == 0, low, jnp.where(place == SUBLANES - 1, high, inside))

    return each(partner, parts)


def partners(parts, colour):
    return along_columns(parts, colour) if colour < 2 else along_rows(parts, colour)


def pair_table(strengths, colour):
    parts = strengths[colour // 2]
    odd = lax.broadcasted_iota(jnp.int32, parts[0].shape, 2 if colour < 2 else 1) & 1
    holder = odd == colour % 2
    bonds = each(lambda mine, other: jnp.where(holder, mine, other), parts, partners(parts, colour))
    cosh_part = each(lambda bond: 1.0 + (math.cosh(hop_angle) - 1.0) * bond, bonds)
    return cosh_part, each(lambda bond: math.sinh(hop_angle) * bond, bonds)


def apply_pairs(parts, colours, tables):
    for colour in colours:
        mix = lambda mine, other, cosh_part, sinh_part: cosh_part * mine + sinh_part * other
        parts = each(mix, parts, partners(parts, colour), *tables[colour])
    return parts


def last_sign():
    at_end = lax.axis_index("tm") == lax.axis_size("tm") - 1
    return jnp.where(at_end, -1.0, 1.0).astype(jnp.float32)


def halves(value):
    high = value.astype(jnp.bfloat16)
    return high, (value - high.astype(jnp.float32)).astype(jnp.bfloat16)


def const_halves(value):
    high = np.asarray(value, np.float32).astype(jnp.bfloat16)
    low = (value - high.astype(np.float64)).astype(np.float32).astype(jnp.bfloat16)
    return np.stack([high, low])


def product(a, b, dims=ROWS_BY_COLS, cuts=None):
    dot = functools.partial(lax.dot_general, dimension_numbers=dims, preferred_element_type=jnp.float32)
    high, low = a[0], a[1]
    rows = high.shape[0]
    cuts = cuts or [0, rows // 2 // (2 * SUBLANES) * (2 * SUBLANES), rows]
    parts = []
    for start, stop in zip(cuts, cuts[1:]):
        if start < stop:
            both = dot(jnp.concatenate([high[start:stop], low[start:stop]], 0), b[0])
            small = both[stop - start :] + dot(high[start:stop], b[1])
            parts.append(both[: stop - start] + small)
    return jnp.concatenate(parts, 0)


def times(a, b):
    return each(lax.mul, a, b)


def wide(main, halo):
    return each(lambda rows, rim: jnp.concatenate([rows, rim], 0), main, halo)


def local_kernel(phonon, guess, bonds, expo, tables, inner):
    slices = guess.shape[0]
    strengths = [blocks(bonds[d].astype(jnp.float32)) for d in range(2)]
    pairs = [pair_table(strengths, q) for q in range(3)]
    for q in range(3):
        for part in range(2):
            tables[2 * q + part] = joined(pairs[q][part])
    for s in range(slices):
        grown = jnp.exp(-coupling * phonon[s])
        expo[s] = grown
        inner[s] = joined(apply_pairs(blocks(grown * guess[s]), (0, 1, 2), pairs))


class Band:
    def __init__(self, bonds, edges, expo, tables, slices):
        self.tiles = bonds.shape[1] // SUBLANES
        across, down = blocks(edges[2 * slices]), blocks(edges[2 * slices + 1])
        self.pairs = [[blocks(tables[2 * q + part]) for part in range(2)] for q in range(3)]
        self.strip_pairs = [pair_table((across, down), q) for q in range(3)]
        vertical = wide(blocks(bonds[1].astype(jnp.float32)), down)
        self.wide_pairs = {3: pair_table((None, vertical), 3)}
        self.expo = [blocks(expo[s]) for s in range(slices)]
        self.strip_expo = [blocks(jnp.exp(-coupling * edges[slices + s])) for s in range(slices)]

    def own(self, parts):
        return each(lambda part: part[: self.tiles], parts)

    def rim(self, parts):
        return each(lambda part: part[self.tiles :], parts)

    def inner(self, s, field):
        return apply_pairs(times(self.expo[s], field), (0, 1, 2), self.pairs)

    def propagated(self, s, inner, strip):
        strip = apply_pairs(times(self.strip_expo[s], strip), (0, 1, 2), self.strip_pairs)
        return apply_pairs(wide(inner, strip), (3,), self.wide_pairs)

    def pulled(self, field):
        field = self.own(apply_pairs(field, (3,), self.wide_pairs))
        return apply_pairs(field, (2, 1, 0), self.pairs)


def with_following(guess, edges, after, after_edge):
    fields = [wide(blocks(guess[s]), blocks(edges[s])) for s in range(guess.shape[0])]
    sign = last_sign()
    fields.append(each(lambda part: sign * part, wide(blocks(after[0]), blocks(after_edge[0]))))
    return fields


def residual_kernel(source, guess, bonds, edges, after, after_edge, expo, tables, inner, basis, out):
    slices, rows, cols = guess.shape
    band = Band(bonds, edges, expo, tables, slices)
    field = with_following(guess, edges, after, after_edge)
    pieces = []
    link = field[0]
    for s in range(slices):
        applied = band.propagated(s, blocks(inner[s]), blocks(edges[s]))
        following = each(lax.sub, field[s + 1], applied)
        back = joined(times(band.expo[s], band.pulled(following)))
        pieces.append(source[s] - joined(band.own(link)) + back)
        link = following
    pieces.insert(1, joined(band.own(applied)))
    places = [0, slices] + list(range(1, slices))
    for group in (slice(0, 2), slice(2, None)):
        waves = product(basis, halves(jnp.concatenate(pieces[group], 0)), ROWS_BY_ROWS, cuts=[0, cols])
        for i, s in enumerate(places[group]):
            out[:, s * rows : (s + 1) * rows] = waves[:, i * rows : (i + 1) * rows]


def mode_kernel(count, mixed, slices_in, slices_out, rows_in, rows_out, out):
    band, tm, modes, width = mixed.shape
    size = tm * modes
    freqs = slices_in.shape[1] // modes
    length = rows_in.shape[1]
    per = length // band
    slots = width // per
    chunk = slots * modes + 1

    stacked = jnp.concatenate(
        [
            jnp.concatenate(
                [mixed[b, :, :, s * per : (s + 1) * per].reshape(size, per) for b in range(band)], 1
            )
            for s in range(slots)
        ],
        0,
    )
    waves = product(halves(product(slices_in, halves(stacked))), rows_in)

    place = lax.axis_index("band") * tm + lax.axis_index("tm")
    shape = (modes, length)
    column = place * modes + lax.broadcasted_iota(jnp.int32, shape, 0)
    row = lax.broadcasted_iota(jnp.int32, shape, 1)
    sine_c = jnp.sin(((column + 1) // 2).astype(jnp.float32) * (math.pi / count))
    sine_r = jnp.sin(((row + 1) // 2).astype(jnp.float32) * (math.pi / length))
    depth = sine_c * sine_c + sine_r * sine_r
    top = cheb_t(ORDER, 1.0 - depth * (4.0 / half_width))
    gains = []
    for k in range(freqs):
        if k % 2 == 0:
            lift = cheb_slope * (1.0 - math.cos((k + 1) * math.pi / freqs))
            damp = 1.0 / math.cosh(ORDER * math.acosh((cheb_base + lift) / half_width))
            gain = (1.0 - damp * top) / (4.0 * depth + (cheb_base - 4.0 + lift))
        gains.append(gain)
    waves = halves(waves * jnp.concatenate(gains, 0))

    lines = halves(product(rows_out, waves, ROWS_BY_ROWS))
    back = product(slices_out, [part[:length] for part in lines], ROWS_BY_ROWS)
    edge = product([part[length:] for part in lines], slices_out, ROWS_BY_ROWS)[: RIM * band]
    turns = [
        pltpu.roll(edge[:, s * size : (s + 1) * size], RIM * s * modes, 1, stride=modes, stride_axis=0)
        for s in range(slots)
    ]
    group = lax.broadcasted_iota(jnp.int32, (tm, size), 1) // modes
    slot = group - lax.broadcasted_iota(jnp.int32, (tm, size), 0)
    slot = jnp.where(slot < 0, slot + tm, slot)
    for b in range(band):
        rim = jnp.zeros((tm, size), jnp.float32)
        for s in range(slots):
            for q in range(RIM):
                line = turns[s][b * RIM + q : b * RIM + q + 1]
                rim = jnp.where(slot == (RIM * (s + b) + q) % tm, line, rim)
        for p in range(tm):
            at = (b * tm + p) * chunk
            for s in range(slots):
                start = s * size + p * modes
                out[at + s * modes : at + (s + 1) * modes] = back[start : start + modes, b * per : (b + 1) * per]
            out[at + slots * modes : at + chunk] = rim[p : p + 1]


def force_kernel(base, guess, bonds, edges, after, after_edge, expo, tables, mixed, order, sol, mom, turned_edge):
    slices, rows, cols = guess.shape
    devices = lax.axis_size("tm") * lax.axis_size("band")
    modes = cols // devices
    slots = slices + 1
    chunk = slots * modes + 1
    band = Band(bonds, edges, expo, tables, slices)

    rim = mixed[pl.ds(slots * modes, devices, stride=chunk), :]
    lanes = rim.shape[1]
    by = modes * (lax.axis_index("tm") + RIM * lax.axis_index("band"))
    rim = pltpu.roll(rim, lax.rem(2 * lanes - by, lanes), 1)
    turned_edge[...] = rim.T
    groups = lanes // modes
    lines = jnp.concatenate([turned_edge[pl.ds(m, groups, stride=modes), :] for m in range(modes)], 1)
    arrived = [
        jnp.concatenate([mixed[pl.ds(s * modes + m, devices, stride=chunk), :] for m in range(modes)], 0).T
        for s in range(slots)
    ]
    first = lines.shape[0]
    timed = product(halves(jnp.concatenate([lines] + arrived, 0)), order, cuts=[0] + [first + s * rows for s in range(1, slots + 1)])
    strips, timed = timed[:first], timed[first:]

    start = with_following(guess, edges, after, after_edge)
    field = []
    for s in range(slots):
        strip = pltpu.roll(strips[s * RIM : s * RIM + HALO], HALO - NEAR, 0)
        change = wide(blocks(timed[s * rows : (s + 1) * rows]), blocks(strip))
        field.append(each(lambda old, new: old + relaxation * new, start[s], change))
    for s in range(slices):
        own = band.own(field[s])
        ahead = band.propagated(s, band.inner(s, own), band.rim(field[s]))
        pulled = band.pulled(each(lax.sub, field[s + 1], ahead))
        sol[s] = joined(own)
        fermion = (-2.0 * coupling) * joined(times(times(band.expo[s], own), pulled))
        mom[s] = base[s] - step_size * fermion


def call(kernel, outs, *operands, flops=0, **kwargs):
    vmem = pl.BlockSpec(memory_space=pltpu.VMEM)
    return pl.pallas_call(
        kernel,
        out_shape=outs,
        in_specs=[vmem] * len(operands),
        out_specs=jax.tree.map(lambda _: vmem, outs),
        compiler_params=pltpu.CompilerParams(vmem_limit_bytes=12 << 20),
        cost_estimate=pl.CostEstimate(flops=flops, bytes_accessed=4 << 20, transcendentals=0),
        **kwargs,
    )(*map(onchip, operands))


def onchip(value):
    return pltpu.with_memory_space_constraint(value, pltpu.VMEM)


def pack_kernel(guess, *refs):
    last_ph, tops, ends, outs = refs[0], refs[1:4], refs[4:7], refs[7:]
    first, last, rims, rim = outs
    first[...] = guess[...]
    last[...] = last_ph[...]
    early = lax.broadcasted_iota(jnp.int32, tops[0].shape, 1) < EDGE
    at = 0
    for top, end in zip(tops, ends):
        both = jnp.where(early, top[...], end[...]).astype(jnp.float32)
        rims[at : at + top.shape[0]] = both
        if at == 0:
            rim[...] = both[:1]
        at += top.shape[0]


def pack(phonon, guess, bonds):
    slices, rows, cols = guess.shape
    fields = (guess, phonon, bonds)
    last = rows // HALO - 1
    whole = lambda shape: pl.BlockSpec(shape, lambda i: (0, 0, 0))
    tops = [whole((v.shape[0], HALO, cols)) for v in fields]
    ends = [pl.BlockSpec((v.shape[0], HALO, cols), lambda i: (0, last, 0)) for v in fields]
    outs = [(1, rows, cols), (1, rows, cols), (2 * slices + 2, HALO, cols), (1, HALO, cols)]
    final = pl.BlockSpec((1, rows, cols), lambda i: (slices - 1, 0, 0))
    return pl.pallas_call(
        pack_kernel,
        grid=(1,),
        out_shape=[pltpu.VMEM(o, jnp.float32) for o in outs],
        in_specs=[whole((1, rows, cols)), final] + tops + ends,
        out_specs=[whole(o) for o in outs],
    )(guess, phonon, *fields, *fields)


def shards(phonon, momentum, source, guess, bonds):
    slices, rows, cols = guess.shape
    tm, band = lax.axis_size("tm"), lax.axis_size("band")
    total, length, devices = tm * slices, rows * band, tm * band
    modes = cols // devices
    slots = slices + 1

    slot_times = np.concatenate([time_basis(total, slices * np.arange(tm) + s) for s in range(slots)], 1)
    slices_in = np.kron(slot_times, np.eye(modes))
    near = np.concatenate([np.arange(-NEAR, 0), rows + np.arange(NEAR)])
    rim_sites = np.concatenate([(b * rows + near) % length for b in range(band)])
    spare = np.zeros(-len(rim_sites) % (2 * SUBLANES), rim_sites.dtype)
    rows_out = const_halves(space_basis(length, np.concatenate([np.arange(length), rim_sites, spare])).T)
    rows_in = const_halves(space_basis(length, np.arange(length)).T)
    columns = const_halves(space_basis(cols, np.arange(cols)))

    first, last, rims, rim = pack(phonon, guess, bonds)
    edges = band_halo(rims, 0)
    after = shifted(first, 1, 0)
    after_edge = band_halo(rim, 1)

    on = lambda *shape: pltpu.VMEM(shape, jnp.float32)
    expo, tables, inner = call(
        local_kernel, (on(slices, rows, cols), on(6, rows, cols), on(slices, rows, cols)),
        phonon, guess, bonds,
    )
    sent = call(
        residual_kernel, jax.ShapeDtypeStruct((cols, slots * rows), jnp.float32),
        source, guess, bonds, edges, after, after_edge, expo, tables, inner, columns,
    )
    mixed = lax.all_to_all(sent.reshape(devices, modes, slots * rows), EXCHANGE, 0, 0, tiled=True)
    wave_rows = devices * (slots * modes + 1)
    back = call(
        functools.partial(mode_kernel, cols), on(wave_rows, rows),
        mixed.reshape(band, tm, modes, slots * rows),
        const_halves(slices_in), const_halves(np.ascontiguousarray(slices_in.T)), rows_in, rows_out,
    )
    mixed = lax.all_to_all(back.reshape(devices, 1, -1), EXCHANGE, 0, 0, tiled=True)

    after_ph = shifted(phonon[:1], 1, 0)
    before_ph = shifted(last, -1, 0)
    ring = jnp.concatenate([before_ph, phonon, after_ph], 0)
    boson = stiffness * (2.0 * phonon - ring[:-2] - ring[2:]) + mass_term * phonon
    base = momentum - step_size * boson
    like = jax.ShapeDtypeStruct(guess.shape, jnp.float32)
    return call(
        force_kernel, (like, like),
        base, guess, bonds, edges, after, after_edge, expo, tables,
        mixed.reshape(wave_rows, rows),
        np.ascontiguousarray(columns.reshape(2, devices, modes, cols).swapaxes(1, 2).reshape(2, cols, cols)),
        scratch_shapes=[pltpu.VMEM((cols // band, devices), jnp.float32)],
    )


def solution(mesh):
    spec = P("tm", "band", None)
    return jax.shard_map(
        shards,
        mesh=mesh,
        in_specs=(spec, spec, spec, spec, P(None, "band", None)),
        out_specs=(spec, spec),
        check_vma=False,
    )
```

```python
import functools
import math

import numpy as np

import jax
import jax.numpy as jnp
from jax import lax
from jax.experimental import pallas as pl
from jax.experimental.pallas import tpu as pltpu
from jax.sharding import PartitionSpec as P


ORDER = 24

hop_angle = 0.3
coupling = 0.2
stiffness = 1.0
mass_term = 0.5
relaxation = 0.25
step_size = 0.25
cheb_base = 4.03
cheb_slope = 0.5
half_width = 4.0

EDGE = 4
HALO = 2 * EDGE
SUBLANES = 8
LANES = 128
NEAR = 2
RIM = 2 * NEAR
AXES = ("tm", "band")
EXCHANGE = ("band", "tm")
ROWS_BY_COLS = (((1,), (0,)), ((), ()))
ROWS_BY_ROWS = (((1,), (1,)), ((), ()))


def shifted(value, dt, db):
    tm, band = lax.axis_size("tm"), lax.axis_size("band")
    pairs = [
        (((t + dt) % tm) * band + (b + db) % band, t * band + b)
        for t in range(tm)
        for b in range(band)
    ]
    return lax.ppermute(value, AXES, pairs)


def band_halo(tile, dt):
    if lax.axis_size("band") == 2:
        return shifted(tile, dt, 1)
    after = shifted(tile[..., :EDGE, :], dt, 1)
    before = shifted(tile[..., EDGE:, :], dt, -1)
    return jnp.concatenate([after, before], -2)


def time_basis(slices, at):
    k = np.arange(slices)[:, None]
    phase = (2 * (k // 2) + 1) * np.asarray(at)[None, :] % (2 * slices)
    angle = phase * (math.pi / slices)
    return math.sqrt(2.0 / slices) * np.where(k % 2 == 0, np.cos(angle), np.sin(angle))


def space_basis(length, at):
    mode = np.arange(length)[:, None]
    freq = (mode + 1) // 2
    angle = (freq * np.asarray(at)[None, :] % length) * (2.0 * math.pi / length)
    wave = np.where((mode % 2 == 0) & (mode > 0), np.sin(angle), np.cos(angle))
    norm = np.where((mode == 0) | (2 * freq == length), 1.0, 2.0)
    return np.sqrt(norm / length) * wave


def cheb_t(order, x):
    if order == 0:
        return jnp.ones_like(x)
    if order == 1:
        return x
    if order % 2 == 0:
        half = cheb_t(order // 2, x)
        return 2.0 * half * half - 1.0
    return 2.0 * cheb_t((order + 1) // 2, x) * cheb_t(order // 2, x) - x


def blocks(value):
    rows, cols = value.shape
    return [value[:, i : i + LANES].reshape(rows // SUBLANES, SUBLANES, LANES) for i in range(0, cols, LANES)]


def joined(parts):
    return jnp.concatenate([part.reshape(-1, LANES) for part in parts], 1)


def each(function, *lists):
    return [function(*items) for items in zip(*lists)]


def taken(part, index):
    numbers = lax.GatherDimensionNumbers(
        offset_dims=(),
        collapsed_slice_dims=(2,),
        start_index_map=(2,),
        operand_batching_dims=(0, 1),
        start_indices_batching_dims=(0, 1),
    )
    return lax.gather(
        part, index[..., None], numbers, (1, 1, 1), mode=lax.GatherScatterMode.PROMISE_IN_BOUNDS
    )


def along_columns(parts, colour):
    place = lax.broadcasted_iota(jnp.int32, parts[0].shape, 2)
    if colour == 0:
        return each(lambda part: taken(part, place ^ 1), parts)
    before, after = parts[-1:] + parts[:-1], parts[1:] + parts[:1]
    if len(parts) == 2:
        outer = (place == 0) | (place == LANES - 1)
        parts = each(lambda mine, other: jnp.where(outer, other, mine), parts, after)
    else:
        parts = each(
            lambda mine, low, high: jnp.where(place == LANES - 1, low, jnp.where(place == 0, high, mine)),
            parts, before, after,
        )
    index = ((((place + LANES - 1) & (LANES - 1)) ^ 1) + 1) & (LANES - 1)
    return each(lambda part: taken(part, index), parts)


def along_rows(parts, colour):
    place = lax.broadcasted_iota(jnp.int32, parts[0].shape, 1)
    even = (place & 1) == 0

    def partner(part):
        up, down = pltpu.roll(part, SUBLANES - 1, 1), pltpu.roll(part, 1, 1)
        if colour == 2:
            return jnp.where(even, up, down)
        inside = jnp.where(even, down, up)
        if part.shape[0] == 1:
            return inside
        low = jnp.concatenate([down[-1:], down[:-1]], 0)
        high = jnp.concatenate([up[1:], up[:1]], 0)
        return jnp.where(place == 0, low, jnp.where(place == SUBLANES - 1, high, inside))

    return each(partner, parts)


def partners(parts, colour):
    return along_columns(parts, colour) if colour < 2 else along_rows(parts, colour)


def pair_table(strengths, colour):
    parts = strengths[colour // 2]
    odd = lax.broadcasted_iota(jnp.int32, parts[0].shape, 2 if colour < 2 else 1) & 1
    holder = odd == colour % 2
    bonds = each(lambda mine, other: jnp.where(holder, mine, other), parts, partners(parts, colour))
    cosh_part = each(lambda bond: 1.0 + (math.cosh(hop_angle) - 1.0) * bond, bonds)
    return cosh_part, each(lambda bond: math.sinh(hop_angle) * bond, bonds)


def apply_pairs(parts, colours, tables):
    for colour in colours:
        mix = lambda mine, other, cosh_part, sinh_part: cosh_part * mine + sinh_part * other
        parts = each(mix, parts, partners(parts, colour), *tables[colour])
    return parts


def last_sign():
    at_end = lax.axis_index("tm") == lax.axis_size("tm") - 1
    return jnp.where(at_end, -1.0, 1.0).astype(jnp.float32)


def halves(value):
    high = value.astype(jnp.bfloat16)
    return high, (value - high.astype(jnp.float32)).astype(jnp.bfloat16)


def const_halves(value):
    high = np.asarray(value, np.float32).astype(jnp.bfloat16)
    low = (value - high.astype(np.float64)).astype(np.float32).astype(jnp.bfloat16)
    return np.stack([high, low])


def product(a, b, dims=ROWS_BY_COLS, cuts=None):
    dot = functools.partial(lax.dot_general, dimension_numbers=dims, preferred_element_type=jnp.float32)
    high, low = a[0], a[1]
    rows = high.shape[0]
    cuts = cuts or [0, rows // 2 // (2 * SUBLANES) * (2 * SUBLANES), rows]
    parts = []
    for start, stop in zip(cuts, cuts[1:]):
        if start < stop:
            both = dot(jnp.concatenate([high[start:stop], low[start:stop]], 0), b[0])
            small = both[stop - start :] + dot(high[start:stop], b[1])
            parts.append(both[: stop - start] + small)
    return jnp.concatenate(parts, 0)


def times(a, b):
    return each(lax.mul, a, b)


def wide(main, halo):
    return each(lambda rows, rim: jnp.concatenate([rows, rim], 0), main, halo)


def local_kernel(phonon, guess, bonds, expo, tables, inner):
    slices = guess.shape[0]
    strengths = [blocks(bonds[d].astype(jnp.float32)) for d in range(2)]
    pairs = [pair_table(strengths, q) for q in range(3)]
    for q in range(3):
        for part in range(2):
            tables[2 * q + part] = joined(pairs[q][part])
    for s in range(slices):
        grown = jnp.exp(-coupling * phonon[s])
        expo[s] = grown
        inner[s] = joined(apply_pairs(blocks(grown * guess[s]), (0, 1, 2), pairs))


class Band:
    def __init__(self, bonds, edges, expo, tables, slices):
        self.tiles = bonds.shape[1] // SUBLANES
        across, down = blocks(edges[2 * slices]), blocks(edges[2 * slices + 1])
        self.pairs = [[blocks(tables[2 * q + part]) for part in range(2)] for q in range(3)]
        self.strip_pairs = [pair_table((across, down), q) for q in range(3)]
        vertical = wide(blocks(bonds[1].astype(jnp.float32)), down)
        self.wide_pairs = {3: pair_table((None, vertical), 3)}
        self.expo = [blocks(expo[s]) for s in range(slices)]
        self.strip_expo = [blocks(jnp.exp(-coupling * edges[slices + s])) for s in range(slices)]

    def own(self, parts):
        return each(lambda part: part[: self.tiles], parts)

    def rim(self, parts):
        return each(lambda part: part[self.tiles :], parts)

    def inner(self, s, field):
        return apply_pairs(times(self.expo[s], field), (0, 1, 2), self.pairs)

    def propagated(self, s, inner, strip):
        strip = apply_pairs(times(self.strip_expo[s], strip), (0, 1, 2), self.strip_pairs)
        return apply_pairs(wide(inner, strip), (3,), self.wide_pairs)

    def pulled(self, field):
        field = self.own(apply_pairs(field, (3,), self.wide_pairs))
        return apply_pairs(field, (2, 1, 0), self.pairs)


def with_following(guess, edges, after, after_edge):
    fields = [wide(blocks(guess[s]), blocks(edges[s])) for s in range(guess.shape[0])]
    sign = last_sign()
    fields.append(each(lambda part: sign * part, wide(blocks(after[0]), blocks(after_edge[0]))))
    return fields


def residual_kernel(source, guess, bonds, edges, after, after_edge, expo, tables, inner, basis, out):
    slices, rows, cols = guess.shape
    band = Band(bonds, edges, expo, tables, slices)
    field = with_following(guess, edges, after, after_edge)
    pieces = []
    link = field[0]
    for s in range(slices):
        applied = band.propagated(s, blocks(inner[s]), blocks(edges[s]))
        following = each(lax.sub, field[s + 1], applied)
        back = joined(times(band.expo[s], band.pulled(following)))
        pieces.append(source[s] - joined(band.own(link)) + back)
        link = following
    pieces.insert(1, joined(band.own(applied)))
    places = [0, slices] + list(range(1, slices))
    for group in (slice(0, 2), slice(2, None)):
        waves = product(basis, halves(jnp.concatenate(pieces[group], 0)), ROWS_BY_ROWS, cuts=[0, cols])
        for i, s in enumerate(places[group]):
            out[:, s * rows : (s + 1) * rows] = waves[:, i * rows : (i + 1) * rows]


def mode_kernel(count, mixed, slices_in, slices_out, rows_in, rows_out, out):
    band, tm, modes, width = mixed.shape
    size = tm * modes
    freqs = slices_in.shape[1] // modes
    length = rows_in.shape[1]
    per = length // band
    slots = width // per
    chunk = slots * modes + 1

    stacked = jnp.concatenate(
        [
            jnp.concatenate(
                [mixed[b, :, :, s * per : (s + 1) * per].reshape(size, per) for b in range(band)], 1
            )
            for s in range(slots)
        ],
        0,
    )
    waves = product(halves(product(slices_in, halves(stacked))), rows_in)

    place = lax.axis_index("band") * tm + lax.axis_index("tm")
    shape = (modes, length)
    column = place * modes + lax.broadcasted_iota(jnp.int32, shape, 0)
    row = lax.broadcasted_iota(jnp.int32, shape, 1)
    sine_c = jnp.sin(((column + 1) // 2).astype(jnp.float32) * (math.pi / count))
    sine_r = jnp.sin(((row + 1) // 2).astype(jnp.float32) * (math.pi / length))
    depth = sine_c * sine_c + sine_r * sine_r
    top = cheb_t(ORDER, 1.0 - depth * (4.0 / half_width))
    gains = []
    for k in range(freqs):
        if k % 2 == 0:
            lift = cheb_slope * (1.0 - math.cos((k + 1) * math.pi / freqs))
            damp = 1.0 / math.cosh(ORDER * math.acosh((cheb_base + lift) / half_width))
            gain = (1.0 - damp * top) / (4.0 * depth + (cheb_base - 4.0 + lift))
        gains.append(gain)
    waves = halves(waves * jnp.concatenate(gains, 0))

    lines = halves(product(rows_out, waves, ROWS_BY_ROWS))
    back = product(slices_out, [part[:length] for part in lines], ROWS_BY_ROWS)
    edge = product([part[length:] for part in lines], slices_out, ROWS_BY_ROWS)[: RIM * band]
    turns = [
        pltpu.roll(edge[:, s * size : (s + 1) * size], RIM * s * modes, 1, stride=modes, stride_axis=0)
        for s in range(slots)
    ]
    group = lax.broadcasted_iota(jnp.int32, (tm, size), 1) // modes
    slot = group - lax.broadcasted_iota(jnp.int32, (tm, size), 0)
    slot = jnp.where(slot < 0, slot + tm, slot)
    for b in range(band):
        rim = jnp.zeros((tm, size), jnp.float32)
        for s in range(slots):
            for q in range(RIM):
                line = turns[s][b * RIM + q : b * RIM + q + 1]
                rim = jnp.where(slot == (RIM * (s + b) + q) % tm, line, rim)
        for p in range(tm):
            at = (p * band + b) * chunk
            for s in range(slots):
                start = s * size + p * modes
                out[at + s * modes : at + (s + 1) * modes] = back[start : start + modes, b * per : (b + 1) * per]
            out[at + slots * modes : at + chunk] = rim[p : p + 1]


def force_kernel(base, guess, bonds, edges, after, after_edge, expo, tables, mixed, order, sol, mom, turned_edge):
    slices, rows, cols = guess.shape
    devices = lax.axis_size("tm") * lax.axis_size("band")
    modes = cols // devices
    slots = slices + 1
    chunk = slots * modes + 1
    band = Band(bonds, edges, expo, tables, slices)

    rim = mixed[pl.ds(slots * modes, devices, stride=chunk), :]
    lanes = rim.shape[1]
    by = modes * (lax.axis_index("tm") + RIM * lax.axis_index("band"))
    rim = pltpu.roll(rim, lax.rem(2 * lanes - by, lanes), 1)
    turned_edge[...] = rim.T
    groups = lanes // modes
    lines = jnp.concatenate([turned_edge[pl.ds(m, groups, stride=modes), :] for m in range(modes)], 1)
    arrived = [
        jnp.concatenate([mixed[pl.ds(s * modes + m, devices, stride=chunk), :] for m in range(modes)], 0).T
        for s in range(slots)
    ]
    first = lines.shape[0]
    timed = product(halves(jnp.concatenate([lines] + arrived, 0)), order, cuts=[0] + [first + s * rows for s in range(1, slots + 1)])
    strips, timed = timed[:first], timed[first:]

    start = with_following(guess, edges, after, after_edge)
    field = []
    for s in range(slots):
        strip = pltpu.roll(strips[s * RIM : s * RIM + HALO], HALO - NEAR, 0)
        change = wide(blocks(timed[s * rows : (s + 1) * rows]), blocks(strip))
        field.append(each(lambda old, new: old + relaxation * new, start[s], change))
    for s in range(slices):
        own = band.own(field[s])
        ahead = band.propagated(s, band.inner(s, own), band.rim(field[s]))
        pulled = band.pulled(each(lax.sub, field[s + 1], ahead))
        sol[s] = joined(own)
        fermion = (-2.0 * coupling) * joined(times(times(band.expo[s], own), pulled))
        mom[s] = base[s] - step_size * fermion


def call(kernel, outs, *operands, flops=0, **kwargs):
    vmem = pl.BlockSpec(memory_space=pltpu.VMEM)
    return pl.pallas_call(
        kernel,
        out_shape=outs,
        in_specs=[vmem] * len(operands),
        out_specs=jax.tree.map(lambda _: vmem, outs),
        compiler_params=pltpu.CompilerParams(vmem_limit_bytes=12 << 20),
        cost_estimate=pl.CostEstimate(flops=flops, bytes_accessed=4 << 20, transcendentals=0),
        **kwargs,
    )(*map(onchip, operands))


def onchip(value):
    return pltpu.with_memory_space_constraint(value, pltpu.VMEM)


def pack_kernel(guess, *refs):
    last_ph, tops, ends, outs = refs[0], refs[1:4], refs[4:7], refs[7:]
    first, last, rims, rim = outs
    first[...] = guess[...]
    last[...] = last_ph[...]
    early = lax.broadcasted_iota(jnp.int32, tops[0].shape, 1) < EDGE
    at = 0
    for top, end in zip(tops, ends):
        both = jnp.where(early, top[...], end[...]).astype(jnp.float32)
        rims[at : at + top.shape[0]] = both
        if at == 0:
            rim[...] = both[:1]
        at += top.shape[0]


def pack(phonon, guess, bonds):
    slices, rows, cols = guess.shape
    fields = (guess, phonon, bonds)
    last = rows // HALO - 1
    whole = lambda shape: pl.BlockSpec(shape, lambda i: (0, 0, 0))
    tops = [whole((v.shape[0], HALO, cols)) for v in fields]
    ends = [pl.BlockSpec((v.shape[0], HALO, cols), lambda i: (0, last, 0)) for v in fields]
    outs = [(1, rows, cols), (1, rows, cols), (2 * slices + 2, HALO, cols), (1, HALO, cols)]
    final = pl.BlockSpec((1, rows, cols), lambda i: (slices - 1, 0, 0))
    return pl.pallas_call(
        pack_kernel,
        grid=(1,),
        out_shape=[pltpu.VMEM(o, jnp.float32) for o in outs],
        in_specs=[whole((1, rows, cols)), final] + tops + ends,
        out_specs=[whole(o) for o in outs],
    )(guess, phonon, *fields, *fields)


def shards(phonon, momentum, source, guess, bonds):
    slices, rows, cols = guess.shape
    tm, band = lax.axis_size("tm"), lax.axis_size("band")
    total, length, devices = tm * slices, rows * band, tm * band
    modes = cols // devices
    slots = slices + 1

    slot_times = np.concatenate([time_basis(total, slices * np.arange(tm) + s) for s in range(slots)], 1)
    slices_in = np.kron(slot_times, np.eye(modes))
    near = np.concatenate([np.arange(-NEAR, 0), rows + np.arange(NEAR)])
    rim_sites = np.concatenate([(b * rows + near) % length for b in range(band)])
    spare = np.zeros(-len(rim_sites) % (2 * SUBLANES), rim_sites.dtype)
    rows_out = const_halves(space_basis(length, np.concatenate([np.arange(length), rim_sites, spare])).T)
    rows_in = const_halves(space_basis(length, np.arange(length)).T)
    columns = const_halves(space_basis(cols, np.arange(cols)))

    first, last, rims, rim = pack(phonon, guess, bonds)
    edges = band_halo(rims, 0)
    after = shifted(first, 1, 0)
    after_edge = band_halo(rim, 1)

    on = lambda *shape: pltpu.VMEM(shape, jnp.float32)
    expo, tables, inner = call(
        local_kernel, (on(slices, rows, cols), on(6, rows, cols), on(slices, rows, cols)),
        phonon, guess, bonds,
    )
    sent = call(
        residual_kernel, jax.ShapeDtypeStruct((cols, slots * rows), jnp.float32),
        source, guess, bonds, edges, after, after_edge, expo, tables, inner, columns,
    )
    mixed = lax.all_to_all(sent.reshape(devices, modes, slots * rows), EXCHANGE, 0, 0, tiled=True)
    wave_rows = devices * (slots * modes + 1)
    back = call(
        functools.partial(mode_kernel, cols), on(wave_rows, rows),
        mixed.reshape(band, tm, modes, slots * rows),
        const_halves(slices_in), const_halves(np.ascontiguousarray(slices_in.T)), rows_in, rows_out,
    )
    mixed = lax.all_to_all(back.reshape(devices, 1, -1), AXES, 0, 0, tiled=True)

    after_ph = shifted(phonon[:1], 1, 0)
    before_ph = shifted(last, -1, 0)
    ring = jnp.concatenate([before_ph, phonon, after_ph], 0)
    boson = stiffness * (2.0 * phonon - ring[:-2] - ring[2:]) + mass_term * phonon
    base = momentum - step_size * boson
    like = jax.ShapeDtypeStruct(guess.shape, jnp.float32)
    return call(
        force_kernel, (like, like),
        base, guess, bonds, edges, after, after_edge, expo, tables,
        mixed.reshape(wave_rows, rows),
        np.ascontiguousarray(columns.reshape(2, band, tm, modes, cols).swapaxes(1, 2).reshape(2, devices, modes, cols).swapaxes(1, 2).reshape(2, cols, cols)),
        scratch_shapes=[pltpu.VMEM((cols // band, devices), jnp.float32)],
    )


def solution(mesh):
    spec = P("tm", "band", None)
    return jax.shard_map(
        shards,
        mesh=mesh,
        in_specs=(spec, spec, spec, spec, P(None, "band", None)),
        out_specs=(spec, spec),
        check_vma=False,
    )
```

```python
import functools
import math

import numpy as np

import jax
import jax.numpy as jnp
from jax import lax
from jax.experimental import pallas as pl
from jax.experimental.pallas import tpu as pltpu
from jax.sharding import PartitionSpec as P


ORDER = 24

hop_angle = 0.3
coupling = 0.2
stiffness = 1.0
mass_term = 0.5
relaxation = 0.25
step_size = 0.25
cheb_base = 4.03
cheb_slope = 0.5
half_width = 4.0

EDGE = 4
HALO = 2 * EDGE
SUBLANES = 8
LANES = 128
NEAR = 2
RIM = 2 * NEAR
AXES = ("tm", "band")
EXCHANGE = ("band", "tm")
ROWS_BY_COLS = (((1,), (0,)), ((), ()))
ROWS_BY_ROWS = (((1,), (1,)), ((), ()))


def shifted(value, dt, db):
    tm, band = lax.axis_size("tm"), lax.axis_size("band")
    pairs = [
        (((t + dt) % tm) * band + (b + db) % band, t * band + b)
        for t in range(tm)
        for b in range(band)
    ]
    return lax.ppermute(value, AXES, pairs)


def band_halo(tile, dt):
    if lax.axis_size("band") == 2:
        return shifted(tile, dt, 1)
    after = shifted(tile[..., :EDGE, :], dt, 1)
    before = shifted(tile[..., EDGE:, :], dt, -1)
    return jnp.concatenate([after, before], -2)


def time_basis(slices, at):
    k = np.arange(slices)[:, None]
    phase = (2 * (k // 2) + 1) * np.asarray(at)[None, :] % (2 * slices)
    angle = phase * (math.pi / slices)
    return math.sqrt(2.0 / slices) * np.where(k % 2 == 0, np.cos(angle), np.sin(angle))


def space_basis(length, at):
    mode = np.arange(length)[:, None]
    freq = (mode + 1) // 2
    angle = (freq * np.asarray(at)[None, :] % length) * (2.0 * math.pi / length)
    wave = np.where((mode % 2 == 0) & (mode > 0), np.sin(angle), np.cos(angle))
    norm = np.where((mode == 0) | (2 * freq == length), 1.0, 2.0)
    return np.sqrt(norm / length) * wave


def cheb_t(order, x):
    if order == 0:
        return jnp.ones_like(x)
    if order == 1:
        return x
    if order % 2 == 0:
        half = cheb_t(order // 2, x)
        return 2.0 * half * half - 1.0
    return 2.0 * cheb_t((order + 1) // 2, x) * cheb_t(order // 2, x) - x


def blocks(value):
    rows, cols = value.shape
    return [value[:, i : i + LANES].reshape(rows // SUBLANES, SUBLANES, LANES) for i in range(0, cols, LANES)]


def joined(parts):
    return jnp.concatenate([part.reshape(-1, LANES) for part in parts], 1)


def each(function, *lists):
    return [function(*items) for items in zip(*lists)]


def taken(part, index):
    numbers = lax.GatherDimensionNumbers(
        offset_dims=(),
        collapsed_slice_dims=(2,),
        start_index_map=(2,),
        operand_batching_dims=(0, 1),
        start_indices_batching_dims=(0, 1),
    )
    return lax.gather(
        part, index[..., None], numbers, (1, 1, 1), mode=lax.GatherScatterMode.PROMISE_IN_BOUNDS
    )


def along_columns(parts, colour):
    place = lax.broadcasted_iota(jnp.int32, parts[0].shape, 2)
    if colour == 0:
        return each(lambda part: taken(part, place ^ 1), parts)
    before, after = parts[-1:] + parts[:-1], parts[1:] + parts[:1]
    if len(parts) == 2:
        outer = (place == 0) | (place == LANES - 1)
        parts = each(lambda mine, other: jnp.where(outer, other, mine), parts, after)
    else:
        parts = each(
            lambda mine, low, high: jnp.where(place == LANES - 1, low, jnp.where(place == 0, high, mine)),
            parts, before, after,
        )
    index = ((((place + LANES - 1) & (LANES - 1)) ^ 1) + 1) & (LANES - 1)
    return each(lambda part: taken(part, index), parts)


def along_rows(parts, colour):
    place = lax.broadcasted_iota(jnp.int32, parts[0].shape, 1)
    even = (place & 1) == 0

    def partner(part):
        up, down = pltpu.roll(part, SUBLANES - 1, 1), pltpu.roll(part, 1, 1)
        if colour == 2:
            return jnp.where(even, up, down)
        inside = jnp.where(even, down, up)
        if part.shape[0] == 1:
            return inside
        low = jnp.concatenate([down[-1:], down[:-1]], 0)
        high = jnp.concatenate([up[1:], up[:1]], 0)
        return jnp.where(place == 0, low, jnp.where(place == SUBLANES - 1, high, inside))

    return each(partner, parts)


def partners(parts, colour):
    return along_columns(parts, colour) if colour < 2 else along_rows(parts, colour)


def pair_table(strengths, colour):
    parts = strengths[colour // 2]
    odd = lax.broadcasted_iota(jnp.int32, parts[0].shape, 2 if colour < 2 else 1) & 1
    holder = odd == colour % 2
    bonds = each(lambda mine, other: jnp.where(holder, mine, other), parts, partners(parts, colour))
    cosh_part = each(lambda bond: 1.0 + (math.cosh(hop_angle) - 1.0) * bond, bonds)
    return cosh_part, each(lambda bond: math.sinh(hop_angle) * bond, bonds)


def apply_pairs(parts, colours, tables):
    for colour in colours:
        mix = lambda mine, other, cosh_part, sinh_part: cosh_part * mine + sinh_part * other
        parts = each(mix, parts, partners(parts, colour), *tables[colour])
    return parts


def last_sign():
    at_end = lax.axis_index("tm") == lax.axis_size("tm") - 1
    return jnp.where(at_end, -1.0, 1.0).astype(jnp.float32)


def halves(value):
    high = value.astype(jnp.bfloat16)
    return high, (value - high.astype(jnp.float32)).astype(jnp.bfloat16)


def const_halves(value):
    high = np.asarray(value, np.float32).astype(jnp.bfloat16)
    low = (value - high.astype(np.float64)).astype(np.float32).astype(jnp.bfloat16)
    return np.stack([high, low])


def product(a, b, dims=ROWS_BY_COLS, cuts=None):
    dot = functools.partial(lax.dot_general, dimension_numbers=dims, preferred_element_type=jnp.float32)
    high, low = a[0], a[1]
    rows = high.shape[0]
    cuts = cuts or [0, rows // 2 // (2 * SUBLANES) * (2 * SUBLANES), rows]
    parts = []
    for start, stop in zip(cuts, cuts[1:]):
        if start < stop:
            both = dot(jnp.concatenate([high[start:stop], low[start:stop]], 0), b[0])
            small = both[stop - start :] + dot(high[start:stop], b[1])
            parts.append(both[: stop - start] + small)
    return jnp.concatenate(parts, 0)


def times(a, b):
    return each(lax.mul, a, b)


def wide(main, halo):
    return each(lambda rows, rim: jnp.concatenate([rows, rim], 0), main, halo)


def local_kernel(phonon, guess, bonds, expo, tables, inner):
    slices = guess.shape[0]
    strengths = [blocks(bonds[d].astype(jnp.float32)) for d in range(2)]
    pairs = [pair_table(strengths, q) for q in range(3)]
    for q in range(3):
        for part in range(2):
            tables[2 * q + part] = joined(pairs[q][part])
    for s in range(slices):
        grown = jnp.exp(-coupling * phonon[s])
        expo[s] = grown
        inner[s] = joined(apply_pairs(blocks(grown * guess[s]), (0, 1, 2), pairs))


class Band:
    def __init__(self, bonds, edges, expo, tables, slices):
        self.tiles = bonds.shape[1] // SUBLANES
        across, down = blocks(edges[2 * slices]), blocks(edges[2 * slices + 1])
        self.pairs = [[blocks(tables[2 * q + part]) for part in range(2)] for q in range(3)]
        self.strip_pairs = [pair_table((across, down), q) for q in range(3)]
        vertical = wide(blocks(bonds[1].astype(jnp.float32)), down)
        self.wide_pairs = {3: pair_table((None, vertical), 3)}
        self.expo = [blocks(expo[s]) for s in range(slices)]
        self.strip_expo = [blocks(jnp.exp(-coupling * edges[slices + s])) for s in range(slices)]

    def own(self, parts):
        return each(lambda part: part[: self.tiles], parts)

    def rim(self, parts):
        return each(lambda part: part[self.tiles :], parts)

    def inner(self, s, field):
        return apply_pairs(times(self.expo[s], field), (0, 1, 2), self.pairs)

    def propagated(self, s, inner, strip):
        strip = apply_pairs(times(self.strip_expo[s], strip), (0, 1, 2), self.strip_pairs)
        return apply_pairs(wide(inner, strip), (3,), self.wide_pairs)

    def pulled(self, field):
        field = self.own(apply_pairs(field, (3,), self.wide_pairs))
        return apply_pairs(field, (2, 1, 0), self.pairs)


def with_following(guess, edges, after, after_edge):
    fields = [wide(blocks(guess[s]), blocks(edges[s])) for s in range(guess.shape[0])]
    sign = last_sign()
    fields.append(each(lambda part: sign * part, wide(blocks(after[0]), blocks(after_edge[0]))))
    return fields


def residual_kernel(source, guess, bonds, edges, after, after_edge, expo, tables, inner, basis, out):
    slices, rows, cols = guess.shape
    edges = unpaired(edges)
    band = Band(bonds, edges, expo, tables, slices)
    field = with_following(guess, edges, after, after_edge)
    pieces = []
    link = field[0]
    for s in range(slices):
        applied = band.propagated(s, blocks(inner[s]), blocks(edges[s]))
        following = each(lax.sub, field[s + 1], applied)
        back = joined(times(band.expo[s], band.pulled(following)))
        pieces.append(source[s] - joined(band.own(link)) + back)
        link = following
    pieces.insert(1, joined(band.own(applied)))
    places = [0, slices] + list(range(1, slices))
    for group in (slice(0, 2), slice(2, None)):
        waves = product(basis, halves(jnp.concatenate(pieces[group], 0)), ROWS_BY_ROWS, cuts=[0, cols])
        for i, s in enumerate(places[group]):
            out[:, s * rows : (s + 1) * rows] = waves[:, i * rows : (i + 1) * rows]


def mode_kernel(count, mixed, slices_in, slices_out, rows_in, rows_out, out):
    band, tm, modes, width = mixed.shape
    size = tm * modes
    freqs = slices_in.shape[1] // modes
    length = rows_in.shape[1]
    per = length // band
    slots = width // per
    chunk = slots * modes + 1

    stacked = jnp.concatenate(
        [
            jnp.concatenate(
                [mixed[b, :, :, s * per : (s + 1) * per].reshape(size, per) for b in range(band)], 1
            )
            for s in range(slots)
        ],
        0,
    )
    waves = product(halves(product(slices_in, halves(stacked))), rows_in)

    place = lax.axis_index("band") * tm + lax.axis_index("tm")
    shape = (modes, length)
    column = place * modes + lax.broadcasted_iota(jnp.int32, shape, 0)
    row = lax.broadcasted_iota(jnp.int32, shape, 1)
    sine_c = jnp.sin(((column + 1) // 2).astype(jnp.float32) * (math.pi / count))
    sine_r = jnp.sin(((row + 1) // 2).astype(jnp.float32) * (math.pi / length))
    depth = sine_c * sine_c + sine_r * sine_r
    top = cheb_t(ORDER, 1.0 - depth * (4.0 / half_width))
    gains = []
    for k in range(freqs):
        if k % 2 == 0:
            lift = cheb_slope * (1.0 - math.cos((k + 1) * math.pi / freqs))
            damp = 1.0 / math.cosh(ORDER * math.acosh((cheb_base + lift) / half_width))
            gain = (1.0 - damp * top) / (4.0 * depth + (cheb_base - 4.0 + lift))
        gains.append(gain)
    waves = halves(waves * jnp.concatenate(gains, 0))

    lines = halves(product(rows_out, waves, ROWS_BY_ROWS))
    back = product(slices_out, [part[:length] for part in lines], ROWS_BY_ROWS)
    edge = product([part[length:] for part in lines], slices_out, ROWS_BY_ROWS)[: RIM * band]
    turns = [
        pltpu.roll(edge[:, s * size : (s + 1) * size], RIM * s * modes, 1, stride=modes, stride_axis=0)
        for s in range(slots)
    ]
    group = lax.broadcasted_iota(jnp.int32, (tm, size), 1) // modes
    slot = group - lax.broadcasted_iota(jnp.int32, (tm, size), 0)
    slot = jnp.where(slot < 0, slot + tm, slot)
    for b in range(band):
        rim = jnp.zeros((tm, size), jnp.float32)
        for s in range(slots):
            for q in range(RIM):
                line = turns[s][b * RIM + q : b * RIM + q + 1]
                rim = jnp.where(slot == (RIM * (s + b) + q) % tm, line, rim)
        for p in range(tm):
            at = (p * band + b) * chunk
            for s in range(slots):
                start = s * size + p * modes
                out[at + s * modes : at + (s + 1) * modes] = back[start : start + modes, b * per : (b + 1) * per]
            out[at + slots * modes : at + chunk] = rim[p : p + 1]


def force_kernel(base, guess, bonds, edges, after, after_edge, expo, tables, mixed, order, sol, mom, turned_edge):
    slices, rows, cols = guess.shape
    devices = lax.axis_size("tm") * lax.axis_size("band")
    modes = cols // devices
    slots = slices + 1
    chunk = slots * modes + 1
    edges = unpaired(edges)
    band = Band(bonds, edges, expo, tables, slices)

    rim = mixed[pl.ds(slots * modes, devices, stride=chunk), :]
    lanes = rim.shape[1]
    by = modes * (lax.axis_index("tm") + RIM * lax.axis_index("band"))
    rim = pltpu.roll(rim, lax.rem(2 * lanes - by, lanes), 1)
    turned_edge[...] = rim.T
    groups = lanes // modes
    lines = jnp.concatenate([turned_edge[pl.ds(m, groups, stride=modes), :] for m in range(modes)], 1)
    arrived = [
        jnp.concatenate([mixed[pl.ds(s * modes + m, devices, stride=chunk), :] for m in range(modes)], 0).T
        for s in range(slots)
    ]
    first = lines.shape[0]
    timed = product(halves(jnp.concatenate([lines] + arrived, 0)), order, cuts=[0] + [first + s * rows for s in range(1, slots + 1)])
    strips, timed = timed[:first], timed[first:]

    start = with_following(guess, edges, after, after_edge)
    field = []
    for s in range(slots):
        strip = pltpu.roll(strips[s * RIM : s * RIM + HALO], HALO - NEAR, 0)
        change = wide(blocks(timed[s * rows : (s + 1) * rows]), blocks(strip))
        field.append(each(lambda old, new: old + relaxation * new, start[s], change))
    for s in range(slices):
        own = band.own(field[s])
        ahead = band.propagated(s, band.inner(s, own), band.rim(field[s]))
        pulled = band.pulled(each(lax.sub, field[s + 1], ahead))
        sol[s] = joined(own)
        fermion = (-2.0 * coupling) * joined(times(times(band.expo[s], own), pulled))
        mom[s] = base[s] - step_size * fermion


def call(kernel, outs, *operands, flops=0, **kwargs):
    vmem = pl.BlockSpec(memory_space=pltpu.VMEM)
    return pl.pallas_call(
        kernel,
        out_shape=outs,
        in_specs=[vmem] * len(operands),
        out_specs=jax.tree.map(lambda _: vmem, outs),
        compiler_params=pltpu.CompilerParams(vmem_limit_bytes=12 << 20),
        cost_estimate=pl.CostEstimate(flops=flops, bytes_accessed=4 << 20, transcendentals=0),
        **kwargs,
    )(*map(onchip, operands))


def onchip(value):
    return pltpu.with_memory_space_constraint(value, pltpu.VMEM)


def paired(one, two):
    row = lax.broadcasted_iota(jnp.int32, one.shape, 0)
    mine = jnp.where(row < EDGE, one, pltpu.roll(one, HALO - NEAR, 0))
    other = jnp.where(row < EDGE, pltpu.roll(two, NEAR, 0), two)
    return jnp.where((row & NEAR) == 0, mine, other)


def unpaired(edges):
    row = lax.broadcasted_iota(jnp.int32, edges.shape[1:], 0)
    tiles = []
    for i in range(edges.shape[0]):
        tile = edges[i]
        tiles.append(jnp.where(row < EDGE, tile, pltpu.roll(tile, NEAR, 0)))
        tiles.append(jnp.where(row < EDGE, pltpu.roll(tile, HALO - NEAR, 0), tile))
    return tiles


def pack_kernel(guess, *refs):
    last_ph, tops, ends, outs = refs[0], refs[1:4], refs[4:7], refs[7:]
    first, last, rims, rim = outs
    first[...] = guess[...]
    last[...] = last_ph[...]
    early = lax.broadcasted_iota(jnp.int32, tops[0].shape, 1) < EDGE
    at = 0
    for top, end in zip(tops, ends):
        both = jnp.where(early, top[...], end[...]).astype(jnp.float32)
        if at == 0:
            rim[...] = both[:1]
        for s in range(0, both.shape[0], 2):
            rims[at] = paired(both[s], both[s + 1])
            at += 1


def pack(phonon, guess, bonds):
    slices, rows, cols = guess.shape
    fields = (guess, phonon, bonds)
    last = rows // HALO - 1
    whole = lambda shape: pl.BlockSpec(shape, lambda i: (0, 0, 0))
    tops = [whole((v.shape[0], HALO, cols)) for v in fields]
    ends = [pl.BlockSpec((v.shape[0], HALO, cols), lambda i: (0, last, 0)) for v in fields]
    outs = [(1, rows, cols), (1, rows, cols), (slices + 1, HALO, cols), (1, HALO, cols)]
    final = pl.BlockSpec((1, rows, cols), lambda i: (slices - 1, 0, 0))
    return pl.pallas_call(
        pack_kernel,
        grid=(1,),
        out_shape=[pltpu.VMEM(o, jnp.float32) for o in outs],
        in_specs=[whole((1, rows, cols)), final] + tops + ends,
        out_specs=[whole(o) for o in outs],
    )(guess, phonon, *fields, *fields)


def shards(phonon, momentum, source, guess, bonds):
    slices, rows, cols = guess.shape
    tm, band = lax.axis_size("tm"), lax.axis_size("band")
    total, length, devices = tm * slices, rows * band, tm * band
    modes = cols // devices
    slots = slices + 1

    slot_times = np.concatenate([time_basis(total, slices * np.arange(tm) + s) for s in range(slots)], 1)
    slices_in = np.kron(slot_times, np.eye(modes))
    near = np.concatenate([np.arange(-NEAR, 0), rows + np.arange(NEAR)])
    rim_sites = np.concatenate([(b * rows + near) % length for b in range(band)])
    spare = np.zeros(-len(rim_sites) % (2 * SUBLANES), rim_sites.dtype)
    rows_out = const_halves(space_basis(length, np.concatenate([np.arange(length), rim_sites, spare])).T)
    rows_in = const_halves(space_basis(length, np.arange(length)).T)
    columns = const_halves(space_basis(cols, np.arange(cols)))

    first, last, rims, rim = pack(phonon, guess, bonds)
    edges = band_halo(rims, 0)
    after = shifted(first, 1, 0)
    after_edge = band_halo(rim, 1)

    on = lambda *shape: pltpu.VMEM(shape, jnp.float32)
    expo, tables, inner = call(
        local_kernel, (on(slices, rows, cols), on(6, rows, cols), on(slices, rows, cols)),
        phonon, guess, bonds,
    )
    sent = call(
        residual_kernel, jax.ShapeDtypeStruct((cols, slots * rows), jnp.float32),
        source, guess, bonds, edges, after, after_edge, expo, tables, inner, columns,
    )
    mixed = lax.all_to_all(sent.reshape(devices, modes, slots * rows), EXCHANGE, 0, 0, tiled=True)
    wave_rows = devices * (slots * modes + 1)
    back = call(
        functools.partial(mode_kernel, cols), on(wave_rows, rows),
        mixed.reshape(band, tm, modes, slots * rows),
        const_halves(slices_in), const_halves(np.ascontiguousarray(slices_in.T)), rows_in, rows_out,
    )
    mixed = lax.all_to_all(back.reshape(devices, 1, -1), AXES, 0, 0, tiled=True)

    after_ph = shifted(phonon[:1], 1, 0)
    before_ph = shifted(last, -1, 0)
    ring = jnp.concatenate([before_ph, phonon, after_ph], 0)
    boson = stiffness * (2.0 * phonon - ring[:-2] - ring[2:]) + mass_term * phonon
    base = momentum - step_size * boson
    like = jax.ShapeDtypeStruct(guess.shape, jnp.float32)
    return call(
        force_kernel, (like, like),
        base, guess, bonds, edges, after, after_edge, expo, tables,
        mixed.reshape(wave_rows, rows),
        np.ascontiguousarray(columns.reshape(2, band, tm, modes, cols).swapaxes(1, 2).reshape(2, devices, modes, cols).swapaxes(1, 2).reshape(2, cols, cols)),
        scratch_shapes=[pltpu.VMEM((cols // band, devices), jnp.float32)],
    )


def solution(mesh):
    spec = P("tm", "band", None)
    return jax.shard_map(
        shards,
        mesh=mesh,
        in_specs=(spec, spec, spec, spec, P(None, "band", None)),
        out_specs=(spec, spec),
        check_vma=False,
    )
```
